512 devices in a mesh: dp: 16 (over z, x_lo), mp: 32 (over x_hi, y, core).
Axes of the slice: x: 4 (x_hi: 2, x_lo: 2; x = x_hi * 2 + x_lo), y: 8, z: 8, core: 2. Of those that a mesh axis runs over, the one named last changes fastest.
Arguments:
- inputs: bfloat16 [197, 196608], P(None, ('dp', 'mp')), may hold values from -6 to 6
- cotangent: bfloat16 [197, 196608], P(None, ('dp', 'mp')), may hold values from -1.1953125 to 1.1953125
- w_in: bfloat16 [768, 3072], P('dp', 'mp'), may hold values from -0.21875 to 0.21875
- w_out: bfloat16 [3072, 768], P('mp', 'dp'), may hold values from -0.109375 to 0.109375
- prec_in: float32 [768, 3072], P('dp', 'mp'), may hold values from 0.1 to 2
- prec_out: float32 [3072, 768], P('mp', 'dp'), may hold values from 0.1 to 2
Outputs:
- new_prec_in: float32 [768, 3072], P('dp', 'mp')
- new_prec_out: float32 [3072, 768], P('mp', 'dp')
- new_w_in: float32 [768, 3072], P('dp', 'mp')
- new_w_out: float32 [3072, 768], P('mp', 'dp')
The draws below stay inside these ranges and needn't reach their ends.
All inputs are finite; a program needn't handle non-finite values.
Results may differ from the reference program's by a relative error of at most 0.0028.
Values may be sent and summed in bfloat16 or wider, within the bound.
No kernel may reach another device: no remote copies, remote signals or barrier semaphores. Data moves between devices by JAX's collectives and lax.ppermute only.
A program may use at most 64 MiB of HBM per device.

```python
import math
import jax
import jax.numpy as jnp
from jax import lax

D = 768
HID = 3072
SEQ = 197
IMAGES = 256


def shard_levels(own_key, extent, cuts, least, high):
    factor_of = 1.0
    for axis_at, parts in cuts:
        heights = jax.random.uniform(jax.random.fold_in(jax.random.fold_in(own_key, 6), axis_at), (parts,), jnp.float32, least / len(cuts), high / len(cuts))
        factor_of = factor_of * jnp.repeat(jnp.exp(heights), extent[axis_at] // parts).reshape((-1,) + (1,) * (len(extent) - 1 - axis_at))
    return factor_of


def centred(rng, extent, deviation, bound, shards=(), held_as=jnp.bfloat16):
    values = deviation * jax.random.normal(rng, extent, jnp.float32)
    if shards:
        values = values * shard_levels(rng, extent, shards, -0.22, 0.18)
    return jnp.clip(values, -bound, bound).astype(held_as)


def setup_inputs(seed: int = 0) -> dict:
    key_of = jax.random.split(jax.random.key(seed), 7)
    return {
        "inputs": centred(key_of[0], (SEQ, IMAGES * D), 1.0, 6.0, ((1, 512),)),
        "cotangent": centred(key_of[1], (SEQ, IMAGES * D), 0.2, 1.1953125, ((1, 512),)),
        "w_in": centred(key_of[2], (D, HID), D ** -0.5, 0.21875, ((0, 16), (1, 32))),
        "w_out": centred(key_of[3], (HID, D), HID ** -0.5, 0.109375, ((0, 32), (1, 16))),
        "prec_in": jnp.clip(jnp.exp(math.log(2.0) - 2.9957323 * jax.random.uniform(key_of[4], (D, HID), jnp.float32) ** shard_levels(key_of[4], (D, HID), ((0, 16), (1, 32)), -0.2, 0.2)), 0.1, 2.0),
        "prec_out": jnp.clip(jnp.exp(math.log(2.0) - 2.9957323 * jax.random.uniform(key_of[5], (HID, D), jnp.float32) ** shard_levels(key_of[5], (HID, D), ((0, 32), (1, 16)), -0.2, 0.2)), 0.1, 2.0),
    }


def gelu_tanh(v):
    return jax.nn.gelu(v, approximate=True)

def reference(inputs, cotangent, w_in, w_out, prec_in, prec_out):
    images = inputs.shape[1] // D
    inputs3 = jnp.transpose(inputs.reshape(SEQ, images, D), (1, 0, 2))
    cot3 = jnp.transpose(cotangent.reshape(SEQ, images, D), (1, 0, 2))

    def one_image(carry, item):
        sum_in, sq_in, sum_out, sq_out = carry
        rows, grads = item
        pre = jnp.dot(rows, w_in, preferred_element_type=jnp.float32)
        act = gelu_tanh(pre).astype(jnp.bfloat16)
        back = jnp.dot(grads, w_out.T, preferred_element_type=jnp.float32)
        delta = jax.vjp(gelu_tanh, pre)[1](back)[0].astype(jnp.bfloat16)
        g_in = jnp.dot(rows.T, delta, preferred_element_type=jnp.float32)
        g_out = jnp.dot(act.T, grads, preferred_element_type=jnp.float32)
        return ((sum_in + g_in, sq_in + g_in * g_in, sum_out + g_out, sq_out + g_out * g_out), None)
    zeros_in = jnp.zeros((D, HID), jnp.float32)
    zeros_out = jnp.zeros((HID, D), jnp.float32)
    totals, _ = lax.scan(one_image, (zeros_in, zeros_in, zeros_out, zeros_out), (inputs3, cot3))
    sum_in, sq_in, sum_out, sq_out = totals
    scale = 1.0 / images
    new_prec_in = 0.6 * prec_in + 0.4 * sq_in * scale
    new_prec_out = 0.6 * prec_out + 0.4 * sq_out * scale
    win = w_in.astype(jnp.float32)
    wout = w_out.astype(jnp.float32)
    new_w_in = win - 1.0 * (sum_in * scale + 0.1 * win) / (new_prec_in + 0.1)
    new_w_out = wout - 1.0 * (sum_out * scale + 0.1 * wout) / (new_prec_out + 0.1)
    return (new_prec_in, new_prec_out, new_w_in, new_w_out)
```

```python
import functools
import math
import jax
import jax.numpy as jnp
from jax import lax
from jax.experimental import pallas as pl
from jax.experimental.pallas import tpu as pltpu
from jax.sharding import Mesh
from jax.sharding import PartitionSpec as P

AXES = ("z", "xlo", "xhi", "y", "core")
DP = ("z", "xlo")
MP = ("xhi", "y", "core")
GROUP = ("y", "core")
OWNERS = ("xhi", "z", "xlo")
BF16 = jnp.bfloat16
F32 = jnp.float32
ROOT = math.sqrt(2.0 / math.pi)
CUBE = 0.044715


def gelu_parts(v):
    v2 = v * v
    t = jnp.tanh(ROOT * v * (1.0 + CUBE * v2))
    half = 0.5 * (1.0 + t)
    slope = half + 0.5 * v * (1.0 - t * t) * (ROOT * (1.0 + 3.0 * CUBE * v2))
    return v * half, slope


def grads_kernel(x_ref, c_ref, w_in_ref, w_out_ref, out_ref, sum_in, sq_in, sum_out, sq_out):
    step = pl.program_id(0)

    def dot(a, b, dims):
        return lax.dot_general(a, b, (dims, ((), ())), preferred_element_type=F32)

    x = jnp.concatenate([x_ref[0], x_ref[1]], axis=1)
    c = jnp.concatenate([c_ref[0], c_ref[1]], axis=1)
    pre = dot(w_in_ref[...], x, ((1,), (1,)))
    back = dot(w_out_ref[...], c, ((1,), (1,)))
    act, slope = gelu_parts(pre)
    act = act.astype(BF16)
    delta = (back * slope).astype(BF16)
    g_in = dot(delta, x, ((1,), (0,)))
    g_out = dot(act, c, ((1,), (0,)))

    @pl.when(step == 0)
    def _():
        sum_in[...] = g_in
        sq_in[...] = g_in * g_in
        sum_out[...] = g_out
        sq_out[...] = g_out * g_out

    @pl.when(step > 0)
    def _():
        sum_in[...] += g_in
        sq_in[...] += g_in * g_in
        sum_out[...] += g_out
        sq_out[...] += g_out * g_out

    @pl.when(step == pl.num_programs(0) - 1)
    def _():
        width = out_ref.shape[2] // 4
        for h in range(out_ref.shape[0]):
            rows = slice(h * width, (h + 1) * width)
            both = [r[rows, :] for r in (sum_in, sq_in, sum_out, sq_out)]
            out_ref[h] = jnp.concatenate(both, axis=0).T.astype(BF16)


def grads(x, c, w_in_t, w_out, blocks):
    hid, d = w_in_t.shape
    pieces, seq, part = x.shape
    per = d // part
    image = pl.BlockSpec((per, seq, part), lambda i: (i, 0, 0))
    whole = pl.BlockSpec((hid, d), lambda i: (0, 0))
    shape = (blocks, d, 4 * hid // blocks)
    return pl.pallas_call(
        grads_kernel,
        grid=(pieces // per,),
        in_specs=[image, image, whole, whole],
        out_specs=pl.BlockSpec(shape, lambda i: (0, 0, 0)),
        out_shape=jax.ShapeDtypeStruct(shape, BF16),
        scratch_shapes=[pltpu.VMEM((hid, d), F32)] * 4,
        compiler_params=pltpu.CompilerParams(vmem_limit_bytes=48 << 20),
    )(x, c, w_in_t, w_out)


def per_device(inputs, cotangent, w_in, w_out, prec_in, prec_out):
    d_own, h_own = w_in.shape
    blocks = lax.axis_size("xhi")
    dp = lax.axis_size("z") * lax.axis_size("xlo")
    both = jnp.concatenate([w_in, w_out.T], axis=0)
    weights = lax.all_gather(both, OWNERS)
    weights = weights.reshape(blocks, dp, 2, d_own, h_own).transpose(2, 0, 4, 1, 3)
    weights = weights.reshape(2, blocks * h_own, dp * d_own)
    x = lax.all_gather(inputs, GROUP)
    c = lax.all_gather(cotangent, GROUP)
    partial = grads(x, c, weights[0], weights[1], blocks)
    pieces = partial.reshape(blocks * dp, d_own, 4 * h_own)
    pieces = lax.all_to_all(pieces, OWNERS, 0, 0, tiled=True)
    total = jnp.sum(pieces.astype(F32), axis=0)
    sum_in, sq_in, sum_out, sq_out = jnp.split(total, 4, axis=1)
    images = x.shape[0] * x.shape[2] // (dp * d_own) * blocks * dp
    scale = 1.0 / images
    new_prec_in = 0.6 * prec_in + 0.4 * sq_in * scale
    new_prec_out = 0.6 * prec_out + 0.4 * sq_out.T * scale
    w_in_own = w_in.astype(F32)
    w_out_own = w_out.astype(F32)
    new_w_in = w_in_own - 1.0 * (sum_in * scale + 0.1 * w_in_own) / (new_prec_in + 0.1)
    new_w_out = w_out_own - 1.0 * (sum_out.T * scale + 0.1 * w_out_own) / (new_prec_out + 0.1)
    return (new_prec_in, new_prec_out, new_w_in, new_w_out)


def solution(mesh):
    torus = Mesh(mesh.devices.reshape(8, 2, 2, 8, 2), AXES)
    dp_mp = DP + MP
    in_specs = (P(None, dp_mp), P(None, dp_mp), P(DP, MP), P(MP, DP), P(DP, MP), P(MP, DP))
    out_specs = (P(DP, MP), P(MP, DP), P(DP, MP), P(MP, DP))
    return jax.shard_map(
        per_device, mesh=torus, in_specs=in_specs, out_specs=out_specs, check_vma=False
    )
```

```python
import functools
import math
import jax
import jax.numpy as jnp
from jax import lax
from jax.experimental import pallas as pl
from jax.experimental.pallas import tpu as pltpu
from jax.sharding import Mesh
from jax.sharding import PartitionSpec as P

AXES = ("z", "xlo", "xhi", "y", "core")
DP = ("z", "xlo")
MP = ("xhi", "y", "core")
GROUP = ("y", "core")
OWNERS = ("xhi", "z", "xlo")
ROW = ("xhi", "xlo")
BF16 = jnp.bfloat16
F32 = jnp.float32
ROOT = math.sqrt(2.0 / math.pi)
CUBE = 0.044715


def gelu_parts(v):
    v2 = v * v
    t = jnp.tanh(ROOT * v * (1.0 + CUBE * v2))
    half = 0.5 * (1.0 + t)
    slope = half + 0.5 * v * (1.0 - t * t) * (ROOT * (1.0 + 3.0 * CUBE * v2))
    return v * half, slope


def grads_kernel(xc_ref, w_in_ref, w_out_ref, out_ref, sum_in, sq_in, sum_out, sq_out):
    step = pl.program_id(0)

    def dot(a, b, dims):
        return lax.dot_general(a, b, (dims, ((), ())), preferred_element_type=F32)

    x = jnp.concatenate([xc_ref[0, 0], xc_ref[1, 0]], axis=1)
    c = jnp.concatenate([xc_ref[0, 1], xc_ref[1, 1]], axis=1)
    pre = dot(w_in_ref[...], x, ((1,), (1,)))
    back = dot(w_out_ref[...], c, ((1,), (1,)))
    act, slope = gelu_parts(pre)
    act = act.astype(BF16)
    delta = (back * slope).astype(BF16)
    g_in = dot(delta, x, ((1,), (0,)))
    g_out = dot(act, c, ((1,), (0,)))

    @pl.when(step == 0)
    def _():
        sum_in[...] = g_in
        sq_in[...] = g_in * g_in
        sum_out[...] = g_out
        sq_out[...] = g_out * g_out

    @pl.when(step > 0)
    def _():
        sum_in[...] += g_in
        sq_in[...] += g_in * g_in
        sum_out[...] += g_out
        sq_out[...] += g_out * g_out

    @pl.when(step == pl.num_programs(0) - 1)
    def _():
        cols, pairs, deep, rows, packed = out_ref.shape
        width = packed // 4
        for h in range(cols):
            part = slice(h * width, (h + 1) * width)
            both = [r[part, :] for r in (sum_in, sq_in, sum_out, sq_out)]
            turned = jnp.concatenate(both, axis=0).T.astype(BF16)
            for k in range(deep * pairs):
                out_ref[h, k % pairs, k // pairs] = turned[k * rows : (k + 1) * rows]


def grads(xc, w_in_t, w_out, shape):
    hid, d = w_in_t.shape
    pieces, two, seq, part = xc.shape
    per = d // part
    whole = pl.BlockSpec((hid, d), lambda i: (0, 0))
    return pl.pallas_call(
        grads_kernel,
        grid=(pieces // per,),
        in_specs=[pl.BlockSpec((per, two, seq, part), lambda i: (i, 0, 0, 0)), whole, whole],
        out_specs=pl.BlockSpec(shape, lambda i: (0,) * len(shape)),
        out_shape=jax.ShapeDtypeStruct(shape, BF16),
        scratch_shapes=[pltpu.VMEM((hid, d), F32)] * 4,
        compiler_params=pltpu.CompilerParams(vmem_limit_bytes=48 << 20),
    )(xc, w_in_t, w_out)


def per_device(inputs, cotangent, w_in, w_out, prec_in, prec_out):
    d_own, h_own = w_in.shape
    cols, pairs, deep = (lax.axis_size(a) for a in ("xhi", "xlo", "z"))
    dp = deep * pairs
    xc = lax.all_gather(jnp.stack([inputs, cotangent]), GROUP)
    both = jnp.concatenate([w_in, w_out.T], axis=0)
    both = jnp.broadcast_to(both[None], (cols * dp, *both.shape))
    weights = lax.all_to_all(both, OWNERS, 0, 0, tiled=True)
    weights = weights.reshape(cols, dp, 2, d_own, h_own).transpose(2, 0, 4, 1, 3)
    weights = weights.reshape(2, cols * h_own, dp * d_own)
    pieces = grads(xc, weights[0], weights[1], (cols, pairs, deep, d_own, 4 * h_own))
    pieces = lax.all_to_all(pieces.reshape(cols * pairs, deep, d_own, 4 * h_own), ROW, 0, 0, tiled=True)
    pieces = sum(pieces[k].astype(F32) for k in range(cols * pairs)).astype(BF16)
    pieces = lax.all_to_all(pieces, "z", 0, 0, tiled=True)
    total = jnp.sum(pieces.astype(F32), axis=0)
    sum_in, sq_in, sum_out, sq_out = jnp.split(total, 4, axis=1)
    images = xc.shape[0] * xc.shape[3] // (dp * d_own) * cols * dp
    scale = 1.0 / images
    new_prec_in = 0.6 * prec_in + 0.4 * sq_in * scale
    new_prec_out = 0.6 * prec_out + 0.4 * sq_out.T * scale
    w_in_own = w_in.astype(F32)
    w_out_own = w_out.astype(F32)
    new_w_in = w_in_own - 1.0 * (sum_in * scale + 0.1 * w_in_own) / (new_prec_in + 0.1)
    new_w_out = w_out_own - 1.0 * (sum_out.T * scale + 0.1 * w_out_own) / (new_prec_out + 0.1)
    return (new_prec_in, new_prec_out, new_w_in, new_w_out)


def solution(mesh):
    torus = Mesh(mesh.devices.reshape(8, 2, 2, 8, 2), AXES)
    dp_mp = DP + MP
    in_specs = (P(None, dp_mp), P(None, dp_mp), P(DP, MP), P(MP, DP), P(DP, MP), P(MP, DP))
    out_specs = (P(DP, MP), P(MP, DP), P(DP, MP), P(MP, DP))
    return jax.shard_map(
        per_device, mesh=torus, in_specs=in_specs, out_specs=out_specs, check_vma=False
    )
```

```python
import math
import jax
import jax.numpy as jnp
from jax import lax
from jax.experimental import pallas as pl
from jax.experimental.pallas import tpu as pltpu
from jax.sharding import Mesh
from jax.sharding import PartitionSpec as P

AXES = ("z", "xlo", "xhi", "y", "core")
DP = ("z", "xlo")
MP = ("xhi", "y", "core")
GROUP = ("y", "core")
OWNERS = ("xhi", "z", "xlo")
ROW = ("xhi", "xlo")
BF16 = jnp.bfloat16
F32 = jnp.float32
ROOT = math.sqrt(2.0 / math.pi)
CUBE = 0.044715


def gelu_parts(v):
    v2 = v * v
    t = jnp.tanh(ROOT * v * (1.0 + CUBE * v2))
    half = 0.5 * (1.0 + t)
    slope = half + 0.5 * v * (1.0 - t * t) * (ROOT * (1.0 + 3.0 * CUBE * v2))
    return v * half, slope


def image_grads(core_ref, own_ref, far_ref, w_in_ref, w_out_ref):
    def dot(a, b, dims):
        return lax.dot_general(a, b, (dims, ((), ())), preferred_element_type=F32)

    first = core_ref[0] == 0

    def whole(k):
        own, far = own_ref[k], far_ref[k]
        return jnp.concatenate(
            [jnp.where(first, own, far), jnp.where(first, far, own)], axis=1
        )

    x, c = whole(0), whole(1)
    pre = dot(w_in_ref[...], x, ((1,), (1,)))
    back = dot(w_out_ref[...], c, ((1,), (1,)))
    act, slope = gelu_parts(pre)
    act = act.astype(BF16)
    delta = (back * slope).astype(BF16)
    return dot(delta, x, ((1,), (0,))), dot(act, c, ((1,), (0,)))


def add_image(sums, g_in, g_out):
    for ref, term in zip(sums, (g_in, g_in * g_in, g_out, g_out * g_out)):
        ref[...] += term


def first_kernel(core_ref, own_ref, far_ref, w_in_ref, w_out_ref, *sums):
    @pl.when(pl.program_id(0) == 0)
    def _():
        for ref in sums:
            ref[...] = jnp.zeros_like(ref)

    add_image(sums, *image_grads(core_ref, own_ref, far_ref, w_in_ref, w_out_ref))


def last_kernel(core_ref, own_ref, far_ref, w_in_ref, w_out_ref, s0, s1, s2, s3, out_ref, *sums):
    step = pl.program_id(0)

    @pl.when(step == 0)
    def _():
        for ref, start in zip(sums, (s0, s1, s2, s3)):
            ref[...] = start[...]

    add_image(sums, *image_grads(core_ref, own_ref, far_ref, w_in_ref, w_out_ref))

    @pl.when(step == pl.num_programs(0) - 1)
    def _():
        cols, pairs, deep, rows, packed = out_ref.shape
        width = packed // 4
        for h in range(cols):
            part = slice(h * width, (h + 1) * width)
            turned = jnp.concatenate([r[part, :] for r in sums], axis=0).T.astype(BF16)
            for k in range(deep * pairs):
                out_ref[h, k % pairs, k // pairs] = turned[k * rows : (k + 1) * rows]


def run_images(kernel, core, own, far, w_in_t, w_out, sums, out_shape):
    pieces, seq, part = own.shape
    hid, d = w_in_t.shape
    images = pieces // 2
    last = images - 1
    block = (2, seq, part)
    whole = pl.BlockSpec((hid, d), lambda i: (0, 0))
    final = bool(sums)
    out_specs = (
        pl.BlockSpec(out_shape, lambda i: (0,) * len(out_shape)) if final else [whole] * 4
    )
    outs = (
        jax.ShapeDtypeStruct(out_shape, BF16)
        if final
        else [jax.ShapeDtypeStruct((hid, d), F32)] * 4
    )
    return pl.pallas_call(
        kernel,
        grid=(images,),
        in_specs=[
            pl.BlockSpec(memory_space=pltpu.SMEM),
            pl.BlockSpec(block, lambda i: (i, 0, 0)),
            pl.BlockSpec(block, lambda i: (jnp.where(i < last, i ^ 1, i), 0, 0)),
            whole,
            whole,
        ]
        + [whole] * len(sums),
        out_specs=out_specs,
        out_shape=outs,
        scratch_shapes=[pltpu.VMEM((hid, d), F32)] * (4 if final else 0),
        compiler_params=pltpu.CompilerParams(vmem_limit_bytes=40 << 20),
        cost_estimate=pl.CostEstimate(
            flops=images * 8 * seq * hid * d,
            bytes_accessed=images * 8 * seq * part,
            transcendentals=images * seq * hid,
        ),
    )(core, own, far, w_in_t, w_out, *sums)


def round_the_ring(own, weights):
    n, cores = lax.axis_size("y"), lax.axis_size("core")

    def turned(step):
        return [
            (y * cores + k, (y + (step if k == 0 else -step)) % n * cores + k)
            for y in range(n)
            for k in range(cores)
        ]

    def swap(a):
        pairs = [(y * cores + k, y * cores + 1 - k) for y in range(n) for k in range(cores)]
        return lax.ppermute(a, GROUP, pairs)

    up, down = [own], [own]
    for _ in range(n // 2 - 1):
        up.append(lax.ppermute(up[-1], GROUP, turned(1)))
        down.append(lax.ppermute(down[-1], GROUP, turned(-1)))
    up[3], down[3], weights = lax.optimization_barrier((up[3], down[3], weights))
    opposite = [lax.ppermute(up[3][:1], GROUP, turned(1)), lax.ppermute(down[3][1:], GROUP, turned(-1))]
    early = jnp.concatenate([up[1], down[1], up[2], down[2], own])
    late = jnp.concatenate([up[3], down[3], *opposite])
    return (early, swap(early)), (late, swap(late)), weights


def per_device(inputs, cotangent, w_in, w_out, prec_in, prec_out):
    d_own, h_own = w_in.shape
    cols, pairs, deep = (lax.axis_size(a) for a in ("xhi", "xlo", "z"))
    dp = deep * pairs
    both = jnp.concatenate([w_in, w_out.T], axis=0)
    both = jnp.broadcast_to(both[None], (cols * dp, *both.shape))
    weights = lax.all_to_all(both, OWNERS, 0, 0, tiled=True)
    weights = weights.reshape(cols, dp, 2, d_own, h_own).transpose(2, 0, 4, 1, 3)
    weights = weights.reshape(2, cols * h_own, dp * d_own)
    early, late, weights = round_the_ring(jnp.stack([inputs, cotangent]), weights)
    core = lax.axis_index("core").reshape(1).astype(jnp.int32)
    shape = (cols, pairs, deep, d_own, 4 * h_own)
    sums = run_images(first_kernel, core, *early, weights[0], weights[1], (), shape)
    pieces = run_images(last_kernel, core, *late, weights[0], weights[1], tuple(sums), shape)
    pieces = lax.all_to_all(pieces.reshape(cols * pairs, *shape[2:]), ROW, 0, 0, tiled=True)
    pieces = sum(pieces[k].astype(F32) for k in range(cols * pairs))
    pieces = lax.all_to_all(pieces, "z", 0, 0, tiled=True)
    total = jnp.sum(pieces, axis=0)
    sum_in, sq_in, sum_out, sq_out = jnp.split(total, 4, axis=1)
    scale = 1.0 / (lax.axis_size("y") * cols * dp)
    new_prec_in = 0.6 * prec_in + 0.4 * sq_in * scale
    new_prec_out = 0.6 * prec_out + 0.4 * sq_out.T * scale
    w_in_own = w_in.astype(F32)
    w_out_own = w_out.astype(F32)
    new_w_in = w_in_own - 1.0 * (sum_in * scale + 0.1 * w_in_own) / (new_prec_in + 0.1)
    new_w_out = w_out_own - 1.0 * (sum_out.T * scale + 0.1 * w_out_own) / (new_prec_out + 0.1)
    return (new_prec_in, new_prec_out, new_w_in, new_w_out)


def solution(mesh):
    torus = Mesh(mesh.devices.reshape(8, 2, 2, 8, 2), AXES)
    dp_mp = DP + MP
    in_specs = (P(None, dp_mp), P(None, dp_mp), P(DP, MP), P(MP, DP), P(DP, MP), P(MP, DP))
    out_specs = (P(DP, MP), P(MP, DP), P(DP, MP), P(MP, DP))
    return jax.shard_map(
        per_device, mesh=torus, in_specs=in_specs, out_specs=out_specs, check_vma=False
    )
```

```python
import functools
import math
import jax
import jax.numpy as jnp
from jax import lax
from jax.experimental import pallas as pl
from jax.experimental.pallas import tpu as pltpu
from jax.sharding import Mesh
from jax.sharding import PartitionSpec as P

AXES = ("z", "xlo", "xhi", "y", "core")
DP = ("z", "xlo")
MP = ("xhi", "y", "core")
GROUP = ("y", "core")
OWNERS = ("z", "xlo", "xhi")
STEP = 2
BF16 = jnp.bfloat16
F32 = jnp.float32
ROOT = math.sqrt(2.0 / math.pi)
CUBE = 0.044715


def gelu_parts(v):
    v2 = v * v
    t = jnp.tanh(ROOT * v * (1.0 + CUBE * v2))
    half = 0.5 * (1.0 + t)
    slope = half + 0.5 * v * (1.0 - t * t) * (ROOT * (1.0 + 3.0 * CUBE * v2))
    return v * half, slope


def grads_kernel(xc_ref, w_in_ref, w_out_ref, out_ref, sum_in, sq_in, sum_out, sq_out):
    step = pl.program_id(0)

    def dot(a, b, dims):
        return lax.dot_general(a, b, (dims, ((), ())), preferred_element_type=F32)

    terms = []
    for n in range(STEP):
        x, c = (jnp.concatenate([xc_ref[2 * n, k], xc_ref[2 * n + 1, k]], axis=1) for k in (0, 1))
        pre = dot(w_in_ref[...], x, ((1,), (1,)))
        back = dot(w_out_ref[...], c, ((1,), (1,)))
        act, slope = gelu_parts(pre)
        act = act.astype(BF16)
        delta = (back * slope).astype(BF16)
        terms.append((dot(delta, x, ((1,), (0,))), dot(act, c, ((1,), (0,)))))
    (g_in, g_out), more = terms[0], terms[1:]
    s_in, s_out = g_in * g_in, g_out * g_out
    for n_in, n_out in more:
        g_in, g_out = g_in + n_in, g_out + n_out
        s_in, s_out = s_in + n_in * n_in, s_out + n_out * n_out

    @pl.when(step == 0)
    def _():
        sum_in[...] = g_in
        sq_in[...] = s_in
        sum_out[...] = g_out
        sq_out[...] = s_out

    @pl.when(step > 0)
    def _():
        sum_in[...] += g_in
        sq_in[...] += s_in
        sum_out[...] += g_out
        sq_out[...] += s_out

    @pl.when(step == pl.num_programs(0) - 1)
    def _():
        blocks, cols, rows, packed = out_ref.shape
        width = packed // 4
        for h in range(cols):
            part = slice(h * width, (h + 1) * width)
            both = [r[part, :] for r in (sum_in, sq_in, sum_out, sq_out)]
            turned = jnp.concatenate(both, axis=0).T.astype(BF16)
            for k in range(blocks):
                out_ref[k, h] = turned[k * rows : (k + 1) * rows]


def grads(xc, w_in_t, w_out, shape):
    hid, d = w_in_t.shape
    pieces, two, seq, part = xc.shape
    per = STEP * d // part
    whole = pl.BlockSpec((hid, d), lambda i: (0, 0))
    return pl.pallas_call(
        grads_kernel,
        grid=(pieces // per,),
        in_specs=[pl.BlockSpec((per, two, seq, part), lambda i: (i, 0, 0, 0)), whole, whole],
        out_specs=pl.BlockSpec(shape, lambda i: (0,) * len(shape)),
        out_shape=jax.ShapeDtypeStruct(shape, BF16),
        scratch_shapes=[pltpu.VMEM((hid, d), F32)] * 4,
        compiler_params=pltpu.CompilerParams(vmem_limit_bytes=48 << 20),
    )(xc, w_in_t, w_out)


def per_device(inputs, cotangent, w_in, w_out, prec_in, prec_out):
    d_own, h_own = w_in.shape
    cols, pairs, deep = (lax.axis_size(a) for a in ("xhi", "xlo", "z"))
    dp = deep * pairs
    xc = lax.all_gather(jnp.stack([inputs, cotangent]), GROUP)
    both = jnp.concatenate([w_in, w_out.T], axis=0)
    both = jnp.broadcast_to(both[None], (cols * dp, *both.shape))
    weights = lax.all_to_all(both, OWNERS, 0, 0, tiled=True)
    weights = weights.reshape(dp, cols, 2, d_own, h_own).transpose(2, 1, 4, 0, 3)
    weights = weights.reshape(2, cols * h_own, dp * d_own)
    pieces = grads(xc, weights[0], weights[1], (dp, cols, d_own, 4 * h_own))
    pieces = lax.all_to_all(pieces.reshape(dp * cols, d_own, 4 * h_own), OWNERS, 0, 0, tiled=True)
    total = jnp.sum(pieces.astype(F32), axis=0)
    sum_in, sq_in, sum_out, sq_out = jnp.split(total, 4, axis=1)
    images = xc.shape[0] * xc.shape[3] // (dp * d_own) * cols * dp
    scale = 1.0 / images
    new_prec_in = 0.6 * prec_in + 0.4 * sq_in * scale
    new_prec_out = 0.6 * prec_out + 0.4 * sq_out.T * scale
    w_in_own = w_in.astype(F32)
    w_out_own = w_out.astype(F32)
    new_w_in = w_in_own - 1.0 * (sum_in * scale + 0.1 * w_in_own) / (new_prec_in + 0.1)
    new_w_out = w_out_own - 1.0 * (sum_out.T * scale + 0.1 * w_out_own) / (new_prec_out + 0.1)
    return (new_prec_in, new_prec_out, new_w_in, new_w_out)


def solution(mesh):
    torus = Mesh(mesh.devices.reshape(8, 2, 2, 8, 2), AXES)
    dp_mp = DP + MP
    in_specs = (P(None, dp_mp), P(None, dp_mp), P(DP, MP), P(MP, DP), P(DP, MP), P(MP, DP))
    out_specs = (P(DP, MP), P(MP, DP), P(DP, MP), P(MP, DP))
    return jax.shard_map(
        per_device, mesh=torus, in_specs=in_specs, out_specs=out_specs, check_vma=False
    )
```

```python
import math
import jax
import jax.numpy as jnp
from jax import lax
from jax.experimental import pallas as pl
from jax.experimental.pallas import tpu as pltpu
from jax.sharding import Mesh
from jax.sharding import PartitionSpec as P

AXES = ("z", "xlo", "xhi", "y", "core")
DP = ("z", "xlo")
MP = ("xhi", "y", "core")
GROUP = ("y", "core")
ROW = ("xlo", "xhi")
BF16 = jnp.bfloat16
F32 = jnp.float32
ROOT = math.sqrt(2.0 / math.pi)
CUBE = 0.044715


def gelu_parts(v):
    v2 = v * v
    t = jnp.tanh(ROOT * v * (1.0 + CUBE * v2))
    half = 0.5 * (1.0 + t)
    slope = half + 0.5 * v * (1.0 - t * t) * (ROOT * (1.0 + 3.0 * CUBE * v2))
    return v * half, slope


def image_grads(core_ref, own_ref, far_ref, turned_ref):
    def dot(a, b, dims):
        return lax.dot_general(a, b, (dims, ((), ())), preferred_element_type=F32)

    first = core_ref[0] == 0
    hid = turned_ref.shape[0] // 2

    def whole(k):
        own, far = own_ref[k], far_ref[k]
        return jnp.concatenate(
            [jnp.where(first, own, far), jnp.where(first, far, own)], axis=1
        )

    x, c = whole(0), whole(1)
    pre = dot(turned_ref[:hid], x, ((1,), (1,)))
    back = dot(turned_ref[hid:], c, ((1,), (1,)))
    act, slope = gelu_parts(pre)
    act = act.astype(BF16)
    delta = (back * slope).astype(BF16)
    return dot(delta, x, ((1,), (0,))), dot(act, c, ((1,), (0,)))


def add_image(sums, g_in, g_out):
    for ref, term in zip(sums, (g_in, g_in * g_in, g_out, g_out * g_out)):
        ref[...] += term


def first_kernel(core_ref, own_ref, far_ref, weights_ref, turned_ref, *sums):
    @pl.when(pl.program_id(0) == 0)
    def _():
        turned_ref[...] = weights_ref[...].T
        for ref in sums:
            ref[...] = jnp.zeros_like(ref)

    add_image(sums, *image_grads(core_ref, own_ref, far_ref, turned_ref))


def last_kernel(core_ref, own_ref, far_ref, turned_ref, s0, s1, s2, s3, out_ref, *sums):
    step = pl.program_id(0)

    @pl.when(step == 0)
    def _():
        for ref, start in zip(sums, (s0, s1, s2, s3)):
            ref[...] = start[...]

    add_image(sums, *image_grads(core_ref, own_ref, far_ref, turned_ref))

    @pl.when(step == pl.num_programs(0) - 1)
    def _():
        pairs, cols, deep, rows, packed = out_ref.shape
        width = packed // 4
        for h in range(cols):
            part = slice(h * width, (h + 1) * width)
            turned = jnp.concatenate([r[part, :] for r in sums], axis=0).T.astype(BF16)
            for k in range(deep * pairs):
                out_ref[k % pairs, h, k // pairs] = turned[k * rows : (k + 1) * rows]


def run_images(kernel, core, own, far, weights, sums, outs):
    pieces, seq, part = own.shape
    last = pieces // 2 - 1
    hid, d = outs[-1].shape if sums == () else sums[0].shape
    block = (2, seq, part)

    def whole(a):
        return pl.BlockSpec(a.shape, lambda i: (0,) * len(a.shape))

    return pl.pallas_call(
        kernel,
        grid=(last + 1,),
        in_specs=[
            pl.BlockSpec(memory_space=pltpu.SMEM),
            pl.BlockSpec(block, lambda i: (i, 0, 0)),
            pl.BlockSpec(block, lambda i: (jnp.where(i < last, i ^ 1, i), 0, 0)),
            whole(weights),
        ]
        + [whole(a) for a in sums],
        out_specs=[whole(a) for a in outs],
        out_shape=outs,
        scratch_shapes=[pltpu.VMEM(a.shape, a.dtype) for a in sums],
        compiler_params=pltpu.CompilerParams(vmem_limit_bytes=40 << 20),
        cost_estimate=pl.CostEstimate(
            flops=pieces * 4 * seq * hid * d,
            bytes_accessed=pieces * 4 * seq * part,
            transcendentals=pieces * seq * hid // 2,
        ),
    )(core, own, far, weights, *sums)


def round_the_ring(own, weights):
    n, cores = lax.axis_size("y"), lax.axis_size("core")

    def turned(step):
        return [
            (y * cores + k, (y + (step if k == 0 else -step)) % n * cores + k)
            for y in range(n)
            for k in range(cores)
        ]

    def swap(a):
        pairs = [(y * cores + k, y * cores + 1 - k) for y in range(n) for k in range(cores)]
        return lax.ppermute(a, GROUP, pairs)

    up, down = [own], [own]
    for _ in range(n // 2 - 1):
        up.append(lax.ppermute(up[-1], GROUP, turned(1)))
        down.append(lax.ppermute(down[-1], GROUP, turned(-1)))
    up[3], down[3], weights = lax.optimization_barrier((up[3], down[3], weights))
    opposite = [lax.ppermute(up[3][:1], GROUP, turned(1)), lax.ppermute(down[3][1:], GROUP, turned(-1))]
    early = jnp.concatenate([up[1], down[1], up[2], down[2], own])
    late = jnp.concatenate([up[3], down[3], *opposite])
    return (early, swap(early)), (late, swap(late)), weights


def per_device(inputs, cotangent, w_in, w_out, prec_in, prec_out):
    d_own, h_own = w_in.shape
    cols, pairs, deep = (lax.axis_size(a) for a in ("xhi", "xlo", "z"))
    dp = deep * pairs
    hid = cols * h_own
    both = jnp.concatenate([w_in, w_out.T], axis=1)
    both = jnp.broadcast_to(both[None], (pairs * cols, *both.shape))
    both = lax.all_to_all(both, ROW, 0, 0, tiled=True).reshape(pairs, cols, d_own, 2, h_own)
    both = both.transpose(0, 2, 3, 1, 4).reshape(pairs, d_own, 2 * hid)
    weights = lax.all_to_all(jnp.broadcast_to(both[None], (deep, *both.shape)), "z", 0, 0, tiled=True)
    weights = weights.reshape(dp * d_own, 2 * hid)
    early, late, weights = round_the_ring(jnp.stack([inputs, cotangent]), weights)
    core = lax.axis_index("core").reshape(1).astype(jnp.int32)
    turned = jax.ShapeDtypeStruct((2 * hid, dp * d_own), BF16)
    partial = [jax.ShapeDtypeStruct((hid, dp * d_own), F32)] * 4
    packed = jax.ShapeDtypeStruct((pairs, cols, deep, d_own, 4 * h_own), BF16)
    turned, *partial = run_images(first_kernel, core, *early, weights, (), [turned, *partial])
    (pieces,) = run_images(last_kernel, core, *late, turned, tuple(partial), [packed])
    pieces = pieces.reshape(pairs * cols, deep, d_own, 4 * h_own)
    pieces = lax.all_to_all(pieces, ROW, 0, 0, tiled=True)
    pieces = sum(pieces[k].astype(F32) for k in range(cols * pairs)).astype(BF16)
    pieces = lax.all_to_all(pieces, "z", 0, 0, tiled=True)
    total = jnp.sum(pieces.astype(F32), axis=0)
    sum_in, sq_in, sum_out, sq_out = jnp.split(total, 4, axis=1)
    scale = 1.0 / (lax.axis_size("y") * cols * dp)
    new_prec_in = 0.6 * prec_in + 0.4 * sq_in * scale
    new_prec_out = 0.6 * prec_out + 0.4 * sq_out.T * scale
    w_in_own = w_in.astype(F32)
    w_out_own = w_out.astype(F32)
    new_w_in = w_in_own - 1.0 * (sum_in * scale + 0.1 * w_in_own) / (new_prec_in + 0.1)
    new_w_out = w_out_own - 1.0 * (sum_out.T * scale + 0.1 * w_out_own) / (new_prec_out + 0.1)
    return (new_prec_in, new_prec_out, new_w_in, new_w_out)


def solution(mesh):
    torus = Mesh(mesh.devices.reshape(8, 2, 2, 8, 2), AXES)
    dp_mp = DP + MP
    in_specs = (P(None, dp_mp), P(None, dp_mp), P(DP, MP), P(MP, DP), P(DP, MP), P(MP, DP))
    out_specs = (P(DP, MP), P(MP, DP), P(DP, MP), P(MP, DP))
    return jax.shard_map(
        per_device, mesh=torus, in_specs=in_specs, out_specs=out_specs, check_vma=False
    )
```

```python
import functools
import math
import jax
import jax.numpy as jnp
from jax import lax
from jax.experimental import pallas as pl
from jax.experimental.pallas import tpu as pltpu
from jax.sharding import Mesh
from jax.sharding import PartitionSpec as P

AXES = ("z", "xlo", "xhi", "y", "core")
DP = ("z", "xlo")
MP = ("xhi", "y", "core")
GROUP = ("y", "core")
OWNERS = ("xlo", "xhi", "z")
STEP = 4
BF16 = jnp.bfloat16
F32 = jnp.float32
ROOT = math.sqrt(2.0 / math.pi)
CUBE = 0.044715


def gelu_parts(v):
    v2 = v * v
    t = jnp.tanh(ROOT * v * (1.0 + CUBE * v2))
    half = 0.5 * (1.0 + t)
    slope = half + 0.5 * v * (1.0 - t * t) * (ROOT * (1.0 + 3.0 * CUBE * v2))
    return v * half, slope


def grads_kernel(xc_ref, w_in_ref, w_out_ref, out_ref, sum_in, sq_in, sum_out, sq_out):
    step = pl.program_id(0)

    def dot(a, b, dims):
        return lax.dot_general(a, b, (dims, ((), ())), preferred_element_type=F32)

    terms = []
    for n in range(STEP):
        halves = (xc_ref[2 * n], xc_ref[2 * n + 1])
        part = halves[0].shape[1] // 2
        x = jnp.concatenate([h[:, :part] for h in halves], axis=1)
        c = jnp.concatenate([h[:, part:] for h in halves], axis=1)
        pre = dot(w_in_ref[...], x, ((1,), (1,)))
        back = dot(w_out_ref[...], c, ((1,), (1,)))
        act, slope = gelu_parts(pre)
        act = act.astype(BF16)
        delta = (back * slope).astype(BF16)
        terms.append((dot(delta, x, ((1,), (0,))), dot(act, c, ((1,), (0,)))))
    (g_in, g_out), more = terms[0], terms[1:]
    s_in, s_out = g_in * g_in, g_out * g_out
    for n_in, n_out in more:
        g_in, g_out = g_in + n_in, g_out + n_out
        s_in, s_out = s_in + n_in * n_in, s_out + n_out * n_out

    @pl.when(step == 0)
    def _():
        sum_in[...] = g_in
        sq_in[...] = s_in
        sum_out[...] = g_out
        sq_out[...] = s_out

    @pl.when(step > 0)
    def _():
        sum_in[...] += g_in
        sq_in[...] += s_in
        sum_out[...] += g_out
        sq_out[...] += s_out

    @pl.when(step == pl.num_programs(0) - 1)
    def _():
        pairs, cols, deep, rows, packed = out_ref.shape
        width = packed // 4
        for h in range(cols):
            part = slice(h * width, (h + 1) * width)
            both = [r[part, :] for r in (sum_in, sq_in, sum_out, sq_out)]
            turned = jnp.concatenate(both, axis=0).T.astype(BF16)
            for k in range(deep * pairs):
                out_ref[k % pairs, h, k // pairs] = turned[k * rows : (k + 1) * rows]


def grads(xc, w_in_t, w_out, shape):
    hid, d = w_in_t.shape
    pieces, seq, part = xc.shape
    per = STEP * 2 * d // part
    whole = pl.BlockSpec((hid, d), lambda i: (0, 0))
    return pl.pallas_call(
        grads_kernel,
        grid=(pieces // per,),
        in_specs=[pl.BlockSpec((per, seq, part), lambda i: (i, 0, 0)), whole, whole],
        out_specs=pl.BlockSpec(shape, lambda i: (0,) * len(shape)),
        out_shape=jax.ShapeDtypeStruct(shape, BF16),
        scratch_shapes=[pltpu.VMEM((hid, d), F32)] * 4,
        compiler_params=pltpu.CompilerParams(vmem_limit_bytes=48 << 20),
    )(xc, w_in_t, w_out)


def per_device(inputs, cotangent, w_in, w_out, prec_in, prec_out):
    d_own, h_own = w_in.shape
    cols, pairs, deep = (lax.axis_size(a) for a in ("xhi", "xlo", "z"))
    dp = deep * pairs
    xc = lax.all_gather(jnp.concatenate([inputs, cotangent], axis=1), GROUP)
    both = jnp.concatenate([w_in, w_out.T], axis=0)
    both = jnp.broadcast_to(both[None], (cols * dp, *both.shape))
    weights = lax.all_to_all(both, OWNERS, 0, 0, tiled=True)
    weights = weights.reshape(pairs, cols, deep, 2, d_own, h_own).transpose(3, 1, 5, 2, 0, 4)
    weights = weights.reshape(2, cols * h_own, dp * d_own)
    pieces = grads(xc, weights[0], weights[1], (pairs, cols, deep, d_own, 4 * h_own))
    pieces = lax.all_to_all(pieces.reshape(dp * cols, d_own, 4 * h_own), OWNERS, 0, 0, tiled=True)
    total = jnp.sum(pieces.astype(F32), axis=0)
    sum_in, sq_in, sum_out, sq_out = jnp.split(total, 4, axis=1)
    images = lax.axis_size("y") * cols * dp
    scale = 1.0 / images
    new_prec_in = 0.6 * prec_in + 0.4 * sq_in * scale
    new_prec_out = 0.6 * prec_out + 0.4 * sq_out.T * scale
    w_in_own = w_in.astype(F32)
    w_out_own = w_out.astype(F32)
    new_w_in = w_in_own - 1.0 * (sum_in * scale + 0.1 * w_in_own) / (new_prec_in + 0.1)
    new_w_out = w_out_own - 1.0 * (sum_out.T * scale + 0.1 * w_out_own) / (new_prec_out + 0.1)
    return (new_prec_in, new_prec_out, new_w_in, new_w_out)


def solution(mesh):
    torus = Mesh(mesh.devices.reshape(8, 2, 2, 8, 2), AXES)
    dp_mp = DP + MP
    in_specs = (P(None, dp_mp), P(None, dp_mp), P(DP, MP), P(MP, DP), P(DP, MP), P(MP, DP))
    out_specs = (P(DP, MP), P(MP, DP), P(DP, MP), P(MP, DP))
    return jax.shard_map(
        per_device, mesh=torus, in_specs=in_specs, out_specs=out_specs, check_vma=False
    )
```

```python
import functools
import math
import jax
import jax.numpy as jnp
from jax import lax
from jax.experimental import pallas as pl
from jax.experimental.pallas import tpu as pltpu
from jax.sharding import Mesh
from jax.sharding import PartitionSpec as P

AXES = ("z", "xlo", "xhi", "y", "core")
DP = ("z", "xlo")
MP = ("xhi", "y", "core")
GROUP = ("y", "core")
OWNERS = ("xlo", "xhi", "z")
ROW = ("xlo", "xhi")
STEP = 2
BF16 = jnp.bfloat16
F32 = jnp.float32
ROOT = math.sqrt(2.0 / math.pi)
CUBE = 0.044715


def gelu_parts(v):
    v2 = v * v
    t = jnp.tanh(ROOT * v * (1.0 + CUBE * v2))
    half = 0.5 * (1.0 + t)
    slope = half + 0.5 * v * (1.0 - t * t) * (ROOT * (1.0 + 3.0 * CUBE * v2))
    return v * half, slope


def grads_kernel(xc_ref, w_in_ref, w_out_ref, out_ref, sum_in, sq_in, sum_out, sq_out):
    step = pl.program_id(0)

    def dot(a, b, dims):
        return lax.dot_general(a, b, (dims, ((), ())), preferred_element_type=F32)

    terms = []
    for n in range(STEP):
        halves = (xc_ref[2 * n], xc_ref[2 * n + 1])
        part = halves[0].shape[1] // 2
        x = jnp.concatenate([h[:, :part] for h in halves], axis=1)
        c = jnp.concatenate([h[:, part:] for h in halves], axis=1)
        pre = dot(w_in_ref[...], x, ((1,), (1,)))
        back = dot(w_out_ref[...], c, ((1,), (1,)))
        act, slope = gelu_parts(pre)
        act = act.astype(BF16)
        delta = (back * slope).astype(BF16)
        terms.append((dot(delta, x, ((1,), (0,))), dot(act, c, ((1,), (0,)))))
    (g_in, g_out), more = terms[0], terms[1:]
    s_in, s_out = g_in * g_in, g_out * g_out
    for n_in, n_out in more:
        g_in, g_out = g_in + n_in, g_out + n_out
        s_in, s_out = s_in + n_in * n_in, s_out + n_out * n_out

    @pl.when(step == 0)
    def _():
        sum_in[...] = g_in
        sq_in[...] = s_in
        sum_out[...] = g_out
        sq_out[...] = s_out

    @pl.when(step > 0)
    def _():
        sum_in[...] += g_in
        sq_in[...] += s_in
        sum_out[...] += g_out
        sq_out[...] += s_out

    @pl.when(step == pl.num_programs(0) - 1)
    def _():
        pairs, cols, deep, rows, packed = out_ref.shape
        width = packed // 4
        for h in range(cols):
            part = slice(h * width, (h + 1) * width)
            both = [r[part, :] for r in (sum_in, sq_in, sum_out, sq_out)]
            turned = jnp.concatenate(both, axis=0).T.astype(BF16)
            for k in range(deep * pairs):
                out_ref[k % pairs, h, k // pairs] = turned[k * rows : (k + 1) * rows]


def grads(xc, w_in_t, w_out, shape):
    hid, d = w_in_t.shape
    pieces, seq, part = xc.shape
    per = STEP * 2 * d // part
    whole = pl.BlockSpec((hid, d), lambda i: (0, 0))
    return pl.pallas_call(
        grads_kernel,
        grid=(pieces // per,),
        in_specs=[pl.BlockSpec((per, seq, part), lambda i: (i, 0, 0)), whole, whole],
        out_specs=pl.BlockSpec(shape, lambda i: (0,) * len(shape)),
        out_shape=jax.ShapeDtypeStruct(shape, BF16),
        scratch_shapes=[pltpu.VMEM((hid, d), F32)] * 4,
        compiler_params=pltpu.CompilerParams(vmem_limit_bytes=48 << 20),
    )(xc, w_in_t, w_out)


def update_kernel(pieces_ref, w_in_ref, w_out_ref, prec_in_ref, prec_out_ref, *outs, scale):
    total = pieces_ref[0].astype(F32)
    for k in range(1, pieces_ref.shape[0]):
        total += pieces_ref[k].astype(F32)
    width = w_in_ref.shape[1]
    for n, (w_ref, prec_ref) in enumerate(((w_in_ref, prec_in_ref), (w_out_ref, prec_out_ref))):
        grad = total[:, 2 * n * width : (2 * n + 1) * width]
        square = total[:, (2 * n + 1) * width : (2 * n + 2) * width]
        prec = 0.6 * prec_ref[...] + 0.4 * square * scale
        w = w_ref[...].astype(F32)
        outs[n][...] = prec
        outs[2 + n][...] = w - 1.0 * (grad * scale + 0.1 * w) / (prec + 0.1)


def per_device(inputs, cotangent, w_in, w_out, prec_in, prec_out):
    d_own, h_own = w_in.shape
    cols, pairs, deep = (lax.axis_size(a) for a in ("xhi", "xlo", "z"))
    dp = deep * pairs
    xc = lax.all_gather(jnp.concatenate([inputs, cotangent], axis=1), GROUP)
    both = jnp.concatenate([w_in, w_out.T], axis=0)
    both = jnp.broadcast_to(both[None], (cols * dp, *both.shape))
    weights = lax.all_to_all(both, OWNERS, 0, 0, tiled=True)
    weights = weights.reshape(pairs, cols, deep, 2, d_own, h_own).transpose(3, 1, 5, 2, 0, 4)
    weights = weights.reshape(2, cols * h_own, dp * d_own)
    pieces = grads(xc, weights[0], weights[1], (pairs, cols, deep, d_own, 4 * h_own))
    pieces = pieces.reshape(pairs * cols, deep, d_own, 4 * h_own)
    pieces = lax.all_to_all(pieces, ROW, 0, 0, tiled=True)
    pieces = sum(pieces[k].astype(F32) for k in range(cols * pairs)).astype(BF16)
    pieces = lax.all_to_all(pieces, "z", 0, 0, tiled=True)
    images = lax.axis_size("y") * cols * dp
    new_prec_in, new_prec_out, new_w_in, new_w_out = pl.pallas_call(
        functools.partial(update_kernel, scale=1.0 / images),
        out_shape=[jax.ShapeDtypeStruct((d_own, h_own), F32)] * 4,
    )(pieces, w_in, w_out.T, prec_in, prec_out.T)
    return (new_prec_in, new_prec_out.T, new_w_in, new_w_out.T)


def solution(mesh):
    torus = Mesh(mesh.devices.reshape(8, 2, 2, 8, 2), AXES)
    dp_mp = DP + MP
    in_specs = (P(None, dp_mp), P(None, dp_mp), P(DP, MP), P(MP, DP), P(DP, MP), P(MP, DP))
    out_specs = (P(DP, MP), P(MP, DP), P(DP, MP), P(MP, DP))
    return jax.shard_map(
        per_device, mesh=torus, in_specs=in_specs, out_specs=out_specs, check_vma=False
    )
```

```python
import functools
import math
import jax
import jax.numpy as jnp
from jax import lax
from jax.experimental import pallas as pl
from jax.experimental.pallas import tpu as pltpu
from jax.sharding import Mesh
from jax.sharding import PartitionSpec as P

AXES = ("z", "xlo", "xhi", "y", "core")
DP = ("z", "xlo")
MP = ("xhi", "y", "core")
GROUP = ("y", "core")
OWNERS = ("xlo", "xhi", "z")
ROW = ("xlo", "xhi")
BF16 = jnp.bfloat16
F32 = jnp.float32
ROOT = math.sqrt(2.0 / math.pi)
CUBE = 0.044715
TURN_FLOPS = 1 << 34


def gelu_parts(v):
    v2 = v * v
    t = jnp.tanh(ROOT * v * (1.0 + CUBE * v2))
    half = 0.5 * (1.0 + t)
    slope = half + 0.5 * v * (1.0 - t * t) * (ROOT * (1.0 + 3.0 * CUBE * v2))
    return v * half, slope


def image_grads(core_ref, own_ref, far_ref, turned_ref):
    def dot(a, b, dims):
        return lax.dot_general(a, b, (dims, ((), ())), preferred_element_type=F32)

    first = core_ref[0] == 0
    hid = turned_ref.shape[0] // 2

    def whole(k):
        own, far = own_ref[k], far_ref[k]
        return jnp.concatenate(
            [jnp.where(first, own, far), jnp.where(first, far, own)], axis=1
        )

    x, c = whole(0), whole(1)
    pre = dot(turned_ref[:hid], x, ((1,), (1,)))
    back = dot(turned_ref[hid:], c, ((1,), (1,)))
    act, slope = gelu_parts(pre)
    act = act.astype(BF16)
    delta = (back * slope).astype(BF16)
    return dot(delta, x, ((1,), (0,))), dot(act, c, ((1,), (0,)))


def add_image(sums, g_in, g_out):
    for ref, term in zip(sums, (g_in, g_in * g_in, g_out, g_out * g_out)):
        ref[...] += term


def turn_kernel(arrived_ref, turned_ref, *, pairs, cols, deep):
    own, width = arrived_ref.shape[1] // 2, arrived_ref.shape[2]
    for n in range(2):
        for h in range(cols):
            blocks = [
                arrived_ref[(k % pairs * cols + h) * deep + k // pairs, n * own : (n + 1) * own, :]
                for k in range(deep * pairs)
            ]
            rows = slice((n * cols + h) * width, (n * cols + h + 1) * width)
            turned_ref[rows, :] = jnp.concatenate(blocks, axis=0).T


def first_kernel(core_ref, own_ref, far_ref, turned_ref, *sums):
    @pl.when(pl.program_id(0) == 0)
    def _():
        for ref in sums:
            ref[...] = jnp.zeros_like(ref)

    add_image(sums, *image_grads(core_ref, own_ref, far_ref, turned_ref))


def last_kernel(core_ref, own_ref, far_ref, turned_ref, s0, s1, s2, s3, out_ref, *sums):
    step = pl.program_id(0)

    @pl.when(step == 0)
    def _():
        for ref, start in zip(sums, (s0, s1, s2, s3)):
            ref[...] = start[...]

    add_image(sums, *image_grads(core_ref, own_ref, far_ref, turned_ref))

    @pl.when(step == pl.num_programs(0) - 1)
    def _():
        pairs, cols, deep, rows, packed = out_ref.shape
        width = packed // 4
        for h in range(cols):
            part = slice(h * width, (h + 1) * width)
            turned = jnp.concatenate([r[part, :] for r in sums], axis=0).T.astype(BF16)
            for k in range(deep * pairs):
                out_ref[k % pairs, h, k // pairs] = turned[k * rows : (k + 1) * rows]


def run_images(kernel, core, own, far, weights, sums, outs):
    pieces, seq, part = own.shape
    last = pieces // 2 - 1
    hid, d = outs[0].shape if sums == () else sums[0].shape
    block = (2, seq, part)

    def whole(a):
        return pl.BlockSpec(a.shape, lambda i: (0,) * len(a.shape))

    return pl.pallas_call(
        kernel,
        grid=(last + 1,),
        in_specs=[
            pl.BlockSpec(memory_space=pltpu.SMEM),
            pl.BlockSpec(block, lambda i: (i, 0, 0)),
            pl.BlockSpec(block, lambda i: (jnp.where(i < last, i ^ 1, i), 0, 0)),
            whole(weights),
        ]
        + [whole(a) for a in sums],
        out_specs=[whole(a) for a in outs],
        out_shape=outs,
        scratch_shapes=[pltpu.VMEM(a.shape, a.dtype) for a in sums],
        compiler_params=pltpu.CompilerParams(vmem_limit_bytes=40 << 20),
        cost_estimate=pl.CostEstimate(
            flops=pieces * 4 * seq * hid * d,
            bytes_accessed=pieces * 4 * seq * part,
            transcendentals=pieces * seq * hid // 2,
        ),
    )(core, own, far, weights, *sums)


def round_the_ring(own):
    n, cores = lax.axis_size("y"), lax.axis_size("core")

    def turned(step):
        return [
            (y * cores + k, (y + (step if k == 0 else -step)) % n * cores + k)
            for y in range(n)
            for k in range(cores)
        ]

    def swap(a):
        pairs = [(y * cores + k, y * cores + 1 - k) for y in range(n) for k in range(cores)]
        return lax.ppermute(a, GROUP, pairs)

    up, down = [own], [own]
    for _ in range(n // 2 - 1):
        up.append(lax.ppermute(up[-1], GROUP, turned(1)))
        down.append(lax.ppermute(down[-1], GROUP, turned(-1)))
    opposite = [lax.ppermute(up[3][:1], GROUP, turned(1)), lax.ppermute(down[3][1:], GROUP, turned(-1))]
    early = jnp.concatenate([up[1], down[1], up[2], down[2], own])
    late = jnp.concatenate([up[3], down[3], *opposite])
    return (early, swap(early)), (late, swap(late))


def update_kernel(pieces_ref, w_in_ref, w_out_ref, prec_in_ref, prec_out_ref, *outs, scale):
    total = pieces_ref[0].astype(F32)
    for k in range(1, pieces_ref.shape[0]):
        total += pieces_ref[k].astype(F32)
    width = w_in_ref.shape[1]
    for n, (w_ref, prec_ref) in enumerate(((w_in_ref, prec_in_ref), (w_out_ref, prec_out_ref))):
        grad = total[:, 2 * n * width : (2 * n + 1) * width]
        square = total[:, (2 * n + 1) * width : (2 * n + 2) * width]
        prec = 0.6 * prec_ref[...] + 0.4 * square * scale
        w = w_ref[...].astype(F32)
        outs[n][...] = prec
        outs[2 + n][...] = w - 1.0 * (grad * scale + 0.1 * w) / (prec + 0.1)


def per_device(inputs, cotangent, w_in, w_out, prec_in, prec_out):
    d_own, h_own = w_in.shape
    cols, pairs, deep = (lax.axis_size(a) for a in ("xhi", "xlo", "z"))
    dp = deep * pairs
    hid = cols * h_own
    both = jnp.concatenate([w_in, w_out.T], axis=0)
    both = jnp.broadcast_to(both[None], (cols * dp, *both.shape))
    arrived = lax.all_to_all(both, OWNERS, 0, 0, tiled=True)
    turned = pl.pallas_call(
        functools.partial(turn_kernel, pairs=pairs, cols=cols, deep=deep),
        out_shape=jax.ShapeDtypeStruct((2 * hid, dp * d_own), BF16),
        cost_estimate=pl.CostEstimate(flops=TURN_FLOPS, bytes_accessed=4 * arrived.size, transcendentals=0),
    )(arrived)
    early, late = round_the_ring(jnp.stack([inputs, cotangent]))
    core = lax.axis_index("core").reshape(1).astype(jnp.int32)
    partial = [jax.ShapeDtypeStruct((hid, dp * d_own), F32)] * 4
    packed = jax.ShapeDtypeStruct((pairs, cols, deep, d_own, 4 * h_own), BF16)
    partial = run_images(first_kernel, core, *early, turned, (), partial)
    (pieces,) = run_images(last_kernel, core, *late, turned, tuple(partial), [packed])
    pieces = pieces.reshape(pairs * cols, deep, d_own, 4 * h_own)
    pieces = lax.all_to_all(pieces, ROW, 0, 0, tiled=True)
    pieces = sum(pieces[k].astype(F32) for k in range(cols * pairs)).astype(BF16)
    pieces = lax.all_to_all(pieces, "z", 0, 0, tiled=True)
    images = lax.axis_size("y") * cols * dp
    new_prec_in, new_prec_out, new_w_in, new_w_out = pl.pallas_call(
        functools.partial(update_kernel, scale=1.0 / images),
        out_shape=[jax.ShapeDtypeStruct((d_own, h_own), F32)] * 4,
    )(pieces, w_in, w_out.T, prec_in, prec_out.T)
    return (new_prec_in, new_prec_out.T, new_w_in, new_w_out.T)


def solution(mesh):
    torus = Mesh(mesh.devices.reshape(8, 2, 2, 8, 2), AXES)
    dp_mp = DP + MP
    in_specs = (P(None, dp_mp), P(None, dp_mp), P(DP, MP), P(MP, DP), P(DP, MP), P(MP, DP))
    out_specs = (P(DP, MP), P(MP, DP), P(DP, MP), P(MP, DP))
    return jax.shard_map(
        per_device, mesh=torus, in_specs=in_specs, out_specs=out_specs, check_vma=False
    )
```

```python
import functools
import math
import jax
import jax.numpy as jnp
from jax import lax
from jax.experimental import pallas as pl
from jax.experimental.pallas import tpu as pltpu
from jax.sharding import Mesh
from jax.sharding import PartitionSpec as P

AXES = ("z", "xlo", "xhi", "y", "core")
DP = ("z", "xlo")
MP = ("xhi", "y", "core")
GROUP = ("y", "core")
OWNERS = ("xlo", "xhi", "z")
ROW = ("xlo", "xhi")
BF16 = jnp.bfloat16
F32 = jnp.float32
ROOT = math.sqrt(2.0 / math.pi)
CUBE = 0.044715
TURN_FLOPS = 1 << 34


def gelu_parts(v):
    v2 = v * v
    t = jnp.tanh(ROOT * v * (1.0 + CUBE * v2))
    half = 0.5 * (1.0 + t)
    slope = half + 0.5 * v * (1.0 - t * t) * (ROOT * (1.0 + 3.0 * CUBE * v2))
    return v * half, slope


def summed(core_ref, own_ref, far_ref, turned_ref):
    first = core_ref[0] == 0
    hid = turned_ref.shape[0] // 2
    last = own_ref.shape[0] // 2 - 1

    def dot(a, b, dims):
        return lax.dot_general(a, b, (dims, ((), ())), preferred_element_type=F32)

    def whole(n, k):
        own = own_ref[2 * n + k]
        far = far_ref[2 * (n ^ 1 if n < last else n) + k]
        return jnp.concatenate(
            [jnp.where(first, own, far), jnp.where(first, far, own)], axis=1
        )

    sums = None
    for n in range(last + 1):
        x, c = whole(n, 0), whole(n, 1)
        pre = dot(turned_ref[:hid], x, ((1,), (1,)))
        back = dot(turned_ref[hid:], c, ((1,), (1,)))
        act, slope = gelu_parts(pre)
        act = act.astype(BF16)
        delta = (back * slope).astype(BF16)
        g_in, g_out = dot(delta, x, ((1,), (0,))), dot(act, c, ((1,), (0,)))
        terms = (g_in, g_in * g_in, g_out, g_out * g_out)
        sums = terms if sums is None else tuple(s + t for s, t in zip(sums, terms))
    return sums


def turn_kernel(arrived_ref, turned_ref, *, pairs, cols, deep):
    own, width = arrived_ref.shape[1] // 2, arrived_ref.shape[2]
    for n in range(2):
        for h in range(cols):
            blocks = [
                arrived_ref[(k % pairs * cols + h) * deep + k // pairs, n * own : (n + 1) * own, :]
                for k in range(deep * pairs)
            ]
            rows = slice((n * cols + h) * width, (n * cols + h + 1) * width)
            turned_ref[rows, :] = jnp.concatenate(blocks, axis=0).T


def first_kernel(core_ref, own_ref, far_ref, turned_ref, *sums):
    for ref, term in zip(sums, summed(core_ref, own_ref, far_ref, turned_ref)):
        ref[...] = term


def last_kernel(core_ref, own_ref, far_ref, turned_ref, s0, s1, s2, s3, out_ref):
    sums = summed(core_ref, own_ref, far_ref, turned_ref)
    sums = [ref[...] + term for ref, term in zip((s0, s1, s2, s3), sums)]
    pairs, cols, deep, rows, packed = out_ref.shape
    width = packed // 4
    for h in range(cols):
        part = slice(h * width, (h + 1) * width)
        turned = jnp.concatenate([s[part, :] for s in sums], axis=0).T.astype(BF16)
        for k in range(deep * pairs):
            out_ref[k % pairs, h, k // pairs] = turned[k * rows : (k + 1) * rows]


def run_images(kernel, core, own, far, turned, sums, outs):
    pieces, seq, part = own.shape
    rows, d = turned.shape
    vmem = pl.BlockSpec(memory_space=pltpu.VMEM)
    return pl.pallas_call(
        kernel,
        in_specs=[pl.BlockSpec(memory_space=pltpu.SMEM)] + [vmem] * (3 + len(sums)),
        out_specs=[vmem] * len(outs),
        out_shape=outs,
        compiler_params=pltpu.CompilerParams(vmem_limit_bytes=24 << 20),
        cost_estimate=pl.CostEstimate(
            flops=pieces * 2 * seq * rows * d,
            bytes_accessed=pieces * 4 * seq * part,
            transcendentals=pieces * seq * rows // 4,
        ),
    )(core, own, far, turned, *sums)


def round_the_ring(own, turned_weights):
    n, cores = lax.axis_size("y"), lax.axis_size("core")

    def turned(step):
        return [
            (y * cores + k, (y + (step if k == 0 else -step)) % n * cores + k)
            for y in range(n)
            for k in range(cores)
        ]

    def swap(a):
        pairs = [(y * cores + k, y * cores + 1 - k) for y in range(n) for k in range(cores)]
        return lax.ppermute(a, GROUP, pairs)

    up, down = [own], [own]
    for _ in range(n // 2 - 1):
        up.append(lax.ppermute(up[-1], GROUP, turned(1)))
        down.append(lax.ppermute(down[-1], GROUP, turned(-1)))
    opposite = [lax.ppermute(up[3][:1], GROUP, turned(1)), lax.ppermute(down[3][1:], GROUP, turned(-1))]
    *opposite, turned_weights = lax.optimization_barrier((*opposite, turned_weights))
    early = jnp.concatenate([up[1], down[1], up[2], down[2], own])
    late = jnp.concatenate([up[3], down[3], *opposite])
    return (early, swap(early)), (late, swap(late)), turned_weights


def update_kernel(pieces_ref, w_in_ref, w_out_ref, prec_in_ref, prec_out_ref, *outs, scale):
    total = pieces_ref[0].astype(F32)
    for k in range(1, pieces_ref.shape[0]):
        total += pieces_ref[k].astype(F32)
    width = w_in_ref.shape[1]
    for n, (w_ref, prec_ref) in enumerate(((w_in_ref, prec_in_ref), (w_out_ref, prec_out_ref))):
        grad = total[:, 2 * n * width : (2 * n + 1) * width]
        square = total[:, (2 * n + 1) * width : (2 * n + 2) * width]
        prec = 0.6 * prec_ref[...] + 0.4 * square * scale
        w = w_ref[...].astype(F32)
        outs[n][...] = prec
        outs[2 + n][...] = w - 1.0 * (grad * scale + 0.1 * w) / (prec + 0.1)


def per_device(inputs, cotangent, w_in, w_out, prec_in, prec_out):
    d_own, h_own = w_in.shape
    cols, pairs, deep = (lax.axis_size(a) for a in ("xhi", "xlo", "z"))
    dp = deep * pairs
    hid = cols * h_own
    both = jnp.concatenate([w_in, w_out.T], axis=0)
    both = jnp.broadcast_to(both[None], (cols * dp, *both.shape))
    arrived = lax.all_to_all(both, OWNERS, 0, 0, tiled=True)
    turned = pl.pallas_call(
        functools.partial(turn_kernel, pairs=pairs, cols=cols, deep=deep),
        out_shape=jax.ShapeDtypeStruct((2 * hid, dp * d_own), BF16),

        cost_estimate=pl.CostEstimate(flops=TURN_FLOPS, bytes_accessed=4 * arrived.size, transcendentals=0),
    )(arrived)
    early, late, turned = round_the_ring(jnp.stack([inputs, cotangent]), turned)
    core = lax.axis_index("core").reshape(1).astype(jnp.int32)
    partial = [jax.ShapeDtypeStruct((hid, dp * d_own), F32)] * 4
    packed = jax.ShapeDtypeStruct((pairs, cols, deep, d_own, 4 * h_own), BF16)
    partial = run_images(first_kernel, core, *early, turned, (), partial)
    (pieces,) = run_images(last_kernel, core, *late, turned, tuple(partial), [packed])
    pieces = pieces.reshape(pairs * cols, deep, d_own, 4 * h_own)
    pieces = lax.all_to_all(pieces, ROW, 0, 0, tiled=True)
    pieces = sum(pieces[k].astype(F32) for k in range(cols * pairs)).astype(BF16)
    pieces = lax.all_to_all(pieces, "z", 0, 0, tiled=True)
    images = lax.axis_size("y") * cols * dp
    new_prec_in, new_prec_out, new_w_in, new_w_out = pl.pallas_call(
        functools.partial(update_kernel, scale=1.0 / images),
        out_shape=[jax.ShapeDtypeStruct((d_own, h_own), F32)] * 4,
        compiler_params=pltpu.CompilerParams(vmem_limit_bytes=4 << 20),
    )(pieces, w_in, w_out.T, prec_in, prec_out.T)
    return (new_prec_in, new_prec_out.T, new_w_in, new_w_out.T)


def solution(mesh):
    torus = Mesh(mesh.devices.reshape(8, 2, 2, 8, 2), AXES)
    dp_mp = DP + MP
    in_specs = (P(None, dp_mp), P(None, dp_mp), P(DP, MP), P(MP, DP), P(DP, MP), P(MP, DP))
    out_specs = (P(DP, MP), P(MP, DP), P(DP, MP), P(MP, DP))
    return jax.shard_map(
        per_device, mesh=torus, in_specs=in_specs, out_specs=out_specs, check_vma=False
    )
```

```python
import functools
import math
import jax
import jax.numpy as jnp
from jax import lax
from jax.experimental import pallas as pl
from jax.experimental.pallas import tpu as pltpu
from jax.sharding import Mesh
from jax.sharding import PartitionSpec as P

AXES = ("z", "xlo", "xhi", "y", "core")
DP = ("z", "xlo")
MP = ("xhi", "y", "core")
GROUP = ("y", "core")
OWNERS = ("xlo", "xhi", "z")
ROW = ("xlo", "xhi")
BF16 = jnp.bfloat16
F32 = jnp.float32
ROOT = math.sqrt(2.0 / math.pi)
CUBE = 0.044715
TURN_FLOPS = 1 << 34


def gelu_parts(v):
    v2 = v * v
    t = jnp.tanh(ROOT * v * (1.0 + CUBE * v2))
    half = 0.5 * (1.0 + t)
    slope = half + 0.5 * v * (1.0 - t * t) * (ROOT * (1.0 + 3.0 * CUBE * v2))
    return v * half, slope


def summed(core_ref, own_ref, far_ref, turned_ref):
    first = core_ref[0] == 0
    hid = turned_ref.shape[0] // 2
    last = own_ref.shape[0] // 2 - 1

    def dot(a, b, dims):
        return lax.dot_general(a, b, (dims, ((), ())), preferred_element_type=F32)

    def whole(n, k):
        own = own_ref[2 * n + k]
        far = far_ref[2 * (n ^ 1 if n < last else n) + k]
        return jnp.concatenate(
            [jnp.where(first, own, far), jnp.where(first, far, own)], axis=1
        )

    sums = None
    for n in range(last + 1):
        x, c = whole(n, 0), whole(n, 1)
        pre = dot(turned_ref[:hid], x, ((1,), (1,)))
        back = dot(turned_ref[hid:], c, ((1,), (1,)))
        act, slope = gelu_parts(pre)
        act = act.astype(BF16)
        delta = (back * slope).astype(BF16)
        g_in, g_out = dot(delta, x, ((1,), (0,))), dot(act, c, ((1,), (0,)))
        terms = (g_in, g_in * g_in, g_out, g_out * g_out)
        sums = terms if sums is None else tuple(s + t for s, t in zip(sums, terms))
    return sums


def turn_kernel(arrived_ref, turned_ref, *, pairs, cols, deep):
    own, width = arrived_ref.shape[1] // 2, arrived_ref.shape[2]
    for n in range(2):
        for h in range(cols):
            blocks = [
                arrived_ref[(k % pairs * cols + h) * deep + k // pairs, n * own : (n + 1) * own, :]
                for k in range(deep * pairs)
            ]
            rows = slice((n * cols + h) * width, (n * cols + h + 1) * width)
            turned_ref[rows, :] = jnp.concatenate(blocks, axis=0).T


def first_kernel(core_ref, own_ref, far_ref, turned_ref, *sums):
    for ref, term in zip(sums, summed(core_ref, own_ref, far_ref, turned_ref)):
        ref[...] = term


def last_kernel(core_ref, own_ref, far_ref, turned_ref, s0, s1, s2, s3, out_ref):
    sums = summed(core_ref, own_ref, far_ref, turned_ref)
    sums = [ref[...] + term for ref, term in zip((s0, s1, s2, s3), sums)]
    pairs, cols, deep, rows, packed = out_ref.shape
    width = packed // 4
    for h in range(cols):
        part = slice(h * width, (h + 1) * width)
        turned = jnp.concatenate([s[part, :] for s in sums], axis=0).T.astype(BF16)
        for k in range(deep * pairs):
            out_ref[k % pairs, h, k // pairs] = turned[k * rows : (k + 1) * rows]


def run_images(kernel, core, own, far, turned, sums, outs):
    pieces, seq, part = own.shape
    rows, d = turned.shape
    vmem = pl.BlockSpec(memory_space=pltpu.VMEM)
    return pl.pallas_call(
        kernel,
        in_specs=[pl.BlockSpec(memory_space=pltpu.SMEM)] + [vmem] * (3 + len(sums)),
        out_specs=[vmem] * len(outs),
        out_shape=outs,
        compiler_params=pltpu.CompilerParams(vmem_limit_bytes=24 << 20),
        cost_estimate=pl.CostEstimate(
            flops=pieces * 2 * seq * rows * d,
            bytes_accessed=pieces * 4 * seq * part,
            transcendentals=pieces * seq * rows // 4,
        ),
    )(core, own, far, turned, *sums)


def round_the_ring(own, turned_weights):
    n, cores = lax.axis_size("y"), lax.axis_size("core")

    def turned(step):
        return [
            (y * cores + k, (y + (step if k == 0 else -step)) % n * cores + k)
            for y in range(n)
            for k in range(cores)
        ]

    def swap(a):
        pairs = [(y * cores + k, y * cores + 1 - k) for y in range(n) for k in range(cores)]
        return lax.ppermute(a, GROUP, pairs)

    up, down = [own], [own]
    for _ in range(n // 2 - 1):
        up.append(lax.ppermute(up[-1], GROUP, turned(1)))
        down.append(lax.ppermute(down[-1], GROUP, turned(-1)))
    opposite = [lax.ppermute(up[3][:1], GROUP, turned(1)), lax.ppermute(down[3][1:], GROUP, turned(-1))]

    early = jnp.concatenate([up[1], down[1], up[2], down[2], own])
    late = jnp.concatenate([up[3], down[3], *opposite])
    return (early, swap(early)), (late, swap(late)), turned_weights


def update_kernel(pieces_ref, w_in_ref, w_out_ref, prec_in_ref, prec_out_ref, *outs, scale):
    total = pieces_ref[0].astype(F32)
    for k in range(1, pieces_ref.shape[0]):
        total += pieces_ref[k].astype(F32)
    width = w_in_ref.shape[1]
    for n, (w_ref, prec_ref) in enumerate(((w_in_ref, prec_in_ref), (w_out_ref, prec_out_ref))):
        grad = total[:, 2 * n * width : (2 * n + 1) * width]
        square = total[:, (2 * n + 1) * width : (2 * n + 2) * width]
        prec = 0.6 * prec_ref[...] + 0.4 * square * scale
        w = w_ref[...].astype(F32)
        outs[n][...] = prec
        outs[2 + n][...] = w - 1.0 * (grad * scale + 0.1 * w) / (prec + 0.1)


def per_device(inputs, cotangent, w_in, w_out, prec_in, prec_out):
    d_own, h_own = w_in.shape
    cols, pairs, deep = (lax.axis_size(a) for a in ("xhi", "xlo", "z"))
    dp = deep * pairs
    hid = cols * h_own
    both = jnp.concatenate([w_in, w_out.T], axis=0)
    both = jnp.broadcast_to(both[None], (cols * dp, *both.shape))
    arrived = lax.all_to_all(both, OWNERS, 0, 0, tiled=True)
    turned = pl.pallas_call(
        functools.partial(turn_kernel, pairs=pairs, cols=cols, deep=deep),
        out_shape=jax.ShapeDtypeStruct((2 * hid, dp * d_own), BF16),

        cost_estimate=pl.CostEstimate(flops=TURN_FLOPS, bytes_accessed=4 * arrived.size, transcendentals=0),
    )(arrived)
    early, late, turned = round_the_ring(jnp.stack([inputs, cotangent]), turned)
    core = lax.axis_index("core").reshape(1).astype(jnp.int32)
    partial = [jax.ShapeDtypeStruct((hid, dp * d_own), F32)] * 4
    packed = jax.ShapeDtypeStruct((pairs, cols, deep, d_own, 4 * h_own), BF16)
    partial = run_images(first_kernel, core, *early, turned, (), partial)
    (pieces,) = run_images(last_kernel, core, *late, turned, tuple(partial), [packed])
    pieces = pieces.reshape(pairs * cols, deep, d_own, 4 * h_own)
    pieces = lax.all_to_all(pieces, ROW, 0, 0, tiled=True)
    pieces = sum(pieces[k].astype(F32) for k in range(cols * pairs)).astype(BF16)
    pieces = lax.all_to_all(pieces, "z", 0, 0, tiled=True)
    images = lax.axis_size("y") * cols * dp
    new_prec_in, new_prec_out, new_w_in, new_w_out = pl.pallas_call(
        functools.partial(update_kernel, scale=1.0 / images),
        out_shape=[jax.ShapeDtypeStruct((d_own, h_own), F32)] * 4,
        compiler_params=pltpu.CompilerParams(vmem_limit_bytes=4 << 20),
    )(pieces, w_in, w_out.T, prec_in, prec_out.T)
    return (new_prec_in, new_prec_out.T, new_w_in, new_w_out.T)


def solution(mesh):
    torus = Mesh(mesh.devices.reshape(8, 2, 2, 8, 2), AXES)
    dp_mp = DP + MP
    in_specs = (P(None, dp_mp), P(None, dp_mp), P(DP, MP), P(MP, DP), P(DP, MP), P(MP, DP))
    out_specs = (P(DP, MP), P(MP, DP), P(DP, MP), P(MP, DP))
    return jax.shard_map(
        per_device, mesh=torus, in_specs=in_specs, out_specs=out_specs, check_vma=False
    )
```

```python
import functools
import math
import jax
import jax.numpy as jnp
from jax import lax
from jax.experimental import pallas as pl
from jax.experimental.pallas import tpu as pltpu
from jax.sharding import Mesh
from jax.sharding import PartitionSpec as P

AXES = ("z", "xlo", "xhi", "y", "core")
DP = ("z", "xlo")
MP = ("xhi", "y", "core")
GROUP = ("y", "core")
OWNERS = ("xlo", "xhi", "z")
ROW = ("xlo", "xhi")
BF16 = jnp.bfloat16
F32 = jnp.float32
ROOT = math.sqrt(2.0 / math.pi)
CUBE = 0.044715
TURN_FLOPS = 1 << 34


def gelu_parts(v):
    v2 = v * v
    t = jnp.tanh(ROOT * v * (1.0 + CUBE * v2))
    half = 0.5 * (1.0 + t)
    slope = half + 0.5 * v * (1.0 - t * t) * (ROOT * (1.0 + 3.0 * CUBE * v2))
    return v * half, slope


def summed(core_ref, own_ref, far_ref, turned_ref):
    first = core_ref[0] == 0
    hid = turned_ref.shape[0] // 2
    last = own_ref.shape[0] // 2 - 1

    def dot(a, b, dims):
        return lax.dot_general(a, b, (dims, ((), ())), preferred_element_type=F32)

    def whole(n, k):
        own = own_ref[2 * n + k]
        far = far_ref[2 * (n ^ 1 if n < last else n) + k]
        return jnp.concatenate(
            [jnp.where(first, own, far), jnp.where(first, far, own)], axis=1
        )

    sums = None
    for n in range(last + 1):
        x, c = whole(n, 0), whole(n, 1)
        pre = dot(turned_ref[:hid], x, ((1,), (1,)))
        back = dot(turned_ref[hid:], c, ((1,), (1,)))
        act, slope = gelu_parts(pre)
        act = act.astype(BF16)
        delta = (back * slope).astype(BF16)
        g_in, g_out = dot(delta, x, ((1,), (0,))), dot(act, c, ((1,), (0,)))
        terms = (g_in, g_in * g_in, g_out, g_out * g_out)
        sums = terms if sums is None else tuple(s + t for s, t in zip(sums, terms))
    return sums


def turn_kernel(arrived_ref, turned_ref, *, pairs, cols, deep):
    own, width = arrived_ref.shape[1] // 2, arrived_ref.shape[2]
    for n in range(2):
        for h in range(cols):
            blocks = [
                arrived_ref[(k % pairs * cols + h) * deep + k // pairs, n * own : (n + 1) * own, :]
                for k in range(deep * pairs)
            ]
            rows = slice((n * cols + h) * width, (n * cols + h + 1) * width)
            turned_ref[rows, :] = jnp.concatenate(blocks, axis=0).T


def first_kernel(core_ref, own_ref, far_ref, turned_ref, *sums):
    for ref, term in zip(sums, summed(core_ref, own_ref, far_ref, turned_ref)):
        ref[...] = term


def last_kernel(core_ref, own_ref, far_ref, turned_ref, s0, s1, s2, s3, out_ref):
    sums = summed(core_ref, own_ref, far_ref, turned_ref)
    sums = [ref[...] + term for ref, term in zip((s0, s1, s2, s3), sums)]
    pairs, cols, deep, rows, packed = out_ref.shape
    width = packed // 4
    for h in range(cols):
        part = slice(h * width, (h + 1) * width)
        turned = jnp.concatenate([s[part, :] for s in sums], axis=0).T.astype(BF16)
        for k in range(deep * pairs):
            out_ref[k % pairs, h, k // pairs] = turned[k * rows : (k + 1) * rows]


def run_images(kernel, core, own, far, turned, sums, outs):
    pieces, seq, part = own.shape
    rows, d = turned.shape
    vmem = pl.BlockSpec(memory_space=pltpu.VMEM)
    return pl.pallas_call(
        kernel,
        in_specs=[pl.BlockSpec(memory_space=pltpu.SMEM)] + [vmem] * (3 + len(sums)),
        out_specs=[vmem] * len(outs),
        out_shape=outs,
        compiler_params=pltpu.CompilerParams(vmem_limit_bytes=24 << 20),
        cost_estimate=pl.CostEstimate(
            flops=pieces * 2 * seq * rows * d,
            bytes_accessed=pieces * 4 * seq * part,
            transcendentals=pieces * seq * rows // 4,
        ),
    )(core, own, far, turned, *sums)


def round_the_ring(own, turned_weights):
    n, cores = lax.axis_size("y"), lax.axis_size("core")

    def turned(step):
        return [
            (y * cores + k, (y + (step if k == 0 else -step)) % n * cores + k)
            for y in range(n)
            for k in range(cores)
        ]

    def swap(a):
        pairs = [(y * cores + k, y * cores + 1 - k) for y in range(n) for k in range(cores)]
        return lax.ppermute(a, GROUP, pairs)

    up, down = [own], [own]
    for _ in range(n // 2 - 1):
        up.append(lax.ppermute(up[-1], GROUP, turned(1)))
        down.append(lax.ppermute(down[-1], GROUP, turned(-1)))
    early = jnp.concatenate([up[1], down[1], up[2], down[2], own])
    up[3], down[3], turned_weights, early = lax.optimization_barrier(
        (up[3], down[3], turned_weights, early)
    )
    opposite = [lax.ppermute(up[3][:1], GROUP, turned(1)), lax.ppermute(down[3][1:], GROUP, turned(-1))]

    late = jnp.concatenate([up[3], down[3], *opposite])
    return (early, swap(early)), (late, swap(late)), turned_weights


def update_kernel(pieces_ref, w_in_ref, w_out_ref, prec_in_ref, prec_out_ref, *outs, scale):
    total = pieces_ref[0].astype(F32)
    for k in range(1, pieces_ref.shape[0]):
        total += pieces_ref[k].astype(F32)
    width = w_in_ref.shape[1]
    for n, (w_ref, prec_ref) in enumerate(((w_in_ref, prec_in_ref), (w_out_ref, prec_out_ref))):
        grad = total[:, 2 * n * width : (2 * n + 1) * width]
        square = total[:, (2 * n + 1) * width : (2 * n + 2) * width]
        prec = 0.6 * prec_ref[...] + 0.4 * square * scale
        w = w_ref[...].astype(F32)
        outs[n][...] = prec
        outs[2 + n][...] = w - 1.0 * (grad * scale + 0.1 * w) / (prec + 0.1)


def per_device(inputs, cotangent, w_in, w_out, prec_in, prec_out):
    d_own, h_own = w_in.shape
    cols, pairs, deep = (lax.axis_size(a) for a in ("xhi", "xlo", "z"))
    dp = deep * pairs
    hid = cols * h_own
    both = jnp.concatenate([w_in, w_out.T], axis=0)
    both = jnp.broadcast_to(both[None], (cols * dp, *both.shape))
    arrived = lax.all_to_all(both, OWNERS, 0, 0, tiled=True)
    turned = pl.pallas_call(
        functools.partial(turn_kernel, pairs=pairs, cols=cols, deep=deep),
        out_shape=jax.ShapeDtypeStruct((2 * hid, dp * d_own), BF16),

        compiler_params=pltpu.CompilerParams(vmem_limit_bytes=8 << 20),
        cost_estimate=pl.CostEstimate(flops=TURN_FLOPS, bytes_accessed=4 * arrived.size, transcendentals=0),
    )(arrived)
    early, late, turned = round_the_ring(jnp.stack([inputs, cotangent]), turned)
    core = lax.axis_index("core").reshape(1).astype(jnp.int32)
    partial = [jax.ShapeDtypeStruct((hid, dp * d_own), F32)] * 4
    packed = jax.ShapeDtypeStruct((pairs, cols, deep, d_own, 4 * h_own), BF16)
    partial = run_images(first_kernel, core, *early, turned, (), partial)
    (pieces,) = run_images(last_kernel, core, *late, turned, tuple(partial), [packed])
    pieces = pieces.reshape(pairs * cols, deep, d_own, 4 * h_own)
    pieces = lax.all_to_all(pieces, ROW, 0, 0, tiled=True)
    pieces = sum(pieces[k].astype(F32) for k in range(cols * pairs)).astype(BF16)
    pieces = lax.all_to_all(pieces, "z", 0, 0, tiled=True)
    images = lax.axis_size("y") * cols * dp
    new_prec_in, new_prec_out, new_w_in, new_w_out = pl.pallas_call(
        functools.partial(update_kernel, scale=1.0 / images),
        out_shape=[jax.ShapeDtypeStruct((d_own, h_own), F32)] * 4,
        compiler_params=pltpu.CompilerParams(vmem_limit_bytes=4 << 20),
    )(pieces, w_in, w_out.T, prec_in, prec_out.T)
    return (new_prec_in, new_prec_out.T, new_w_in, new_w_out.T)


def solution(mesh):
    torus = Mesh(mesh.devices.reshape(8, 2, 2, 8, 2), AXES)
    dp_mp = DP + MP
    in_specs = (P(None, dp_mp), P(None, dp_mp), P(DP, MP), P(MP, DP), P(DP, MP), P(MP, DP))
    out_specs = (P(DP, MP), P(MP, DP), P(DP, MP), P(MP, DP))
    return jax.shard_map(
        per_device, mesh=torus, in_specs=in_specs, out_specs=out_specs, check_vma=False
    )
```

```python
import functools
import math
import jax
import jax.numpy as jnp
from jax import lax
from jax.experimental import pallas as pl
from jax.experimental.pallas import tpu as pltpu
from jax.sharding import Mesh
from jax.sharding import PartitionSpec as P

AXES = ("z", "xlo", "xhi", "y", "core")
DP = ("z", "xlo")
MP = ("xhi", "y", "core")
GROUP = ("y", "core")
OWNERS = ("xlo", "xhi", "z")
ROW = ("xlo", "xhi")
BF16 = jnp.bfloat16
F32 = jnp.float32
ROOT = math.sqrt(2.0 / math.pi)
CUBE = 0.044715
TURN_FLOPS = 1 << 34


def gelu_parts(v):
    v2 = v * v
    t = jnp.tanh(ROOT * v * (1.0 + CUBE * v2))
    half = 0.5 * (1.0 + t)
    slope = half + 0.5 * v * (1.0 - t * t) * (ROOT * (1.0 + 3.0 * CUBE * v2))
    return v * half, slope


def summed(core_ref, own_ref, far_ref, turned_ref):
    first = core_ref[0] == 0
    hid = turned_ref.shape[0] // 2
    last = own_ref.shape[0] // 2 - 1

    def dot(a, b, dims):
        return lax.dot_general(a, b, (dims, ((), ())), preferred_element_type=F32)

    def whole(n, k):
        own = own_ref[2 * n + k]
        far = far_ref[2 * (n ^ 1 if n < last else n) + k]
        return jnp.concatenate(
            [jnp.where(first, own, far), jnp.where(first, far, own)], axis=1
        )

    sums = None
    for n in range(last + 1):
        x, c = whole(n, 0), whole(n, 1)
        pre = dot(turned_ref[:hid], x, ((1,), (1,)))
        back = dot(turned_ref[hid:], c, ((1,), (1,)))
        act, slope = gelu_parts(pre)
        act = act.astype(BF16)
        delta = (back * slope).astype(BF16)
        g_in, g_out = dot(delta, x, ((1,), (0,))), dot(act, c, ((1,), (0,)))
        terms = (g_in, g_in * g_in, g_out, g_out * g_out)
        sums = terms if sums is None else tuple(s + t for s, t in zip(sums, terms))
    return sums


def turn_kernel(arrived_ref, turned_ref, *, pairs, cols, deep):
    own, width = arrived_ref.shape[1] // 2, arrived_ref.shape[2]
    for n in range(2):
        for h in range(cols):
            blocks = [
                arrived_ref[(k % pairs * cols + h) * deep + k // pairs, n * own : (n + 1) * own, :]
                for k in range(deep * pairs)
            ]
            rows = slice((n * cols + h) * width, (n * cols + h + 1) * width)
            turned_ref[rows, :] = jnp.concatenate(blocks, axis=0).T


def first_kernel(core_ref, own_ref, far_ref, arrived_ref, turned_ref, *sums, pairs, cols, deep):
    turn_kernel(arrived_ref, turned_ref, pairs=pairs, cols=cols, deep=deep)
    for ref, term in zip(sums, summed(core_ref, own_ref, far_ref, turned_ref)):
        ref[...] = term


def last_kernel(core_ref, own_ref, far_ref, turned_ref, s0, s1, s2, s3, out_ref):
    sums = summed(core_ref, own_ref, far_ref, turned_ref)
    sums = [ref[...] + term for ref, term in zip((s0, s1, s2, s3), sums)]
    pairs, cols, deep, rows, packed = out_ref.shape
    width = packed // 4
    for h in range(cols):
        part = slice(h * width, (h + 1) * width)
        turned = jnp.concatenate([s[part, :] for s in sums], axis=0).T.astype(BF16)
        for k in range(deep * pairs):
            out_ref[k % pairs, h, k // pairs] = turned[k * rows : (k + 1) * rows]


def run_images(kernel, core, own, far, turned, sums, outs):
    pieces, seq, part = own.shape
    rows, d = (outs[0] if sums == () else turned).shape
    vmem = pl.BlockSpec(memory_space=pltpu.VMEM)
    return pl.pallas_call(
        kernel,
        in_specs=[pl.BlockSpec(memory_space=pltpu.SMEM)] + [vmem] * (3 + len(sums)),
        out_specs=[vmem] * len(outs),
        out_shape=outs,
        compiler_params=pltpu.CompilerParams(vmem_limit_bytes=24 << 20),
        cost_estimate=pl.CostEstimate(
            flops=pieces * 2 * seq * rows * d,
            bytes_accessed=pieces * 4 * seq * part,
            transcendentals=pieces * seq * rows // 4,
        ),
    )(core, own, far, turned, *sums)


def round_the_ring(own, turned_weights):
    n, cores = lax.axis_size("y"), lax.axis_size("core")

    def turned(step):
        return [
            (y * cores + k, (y + (step if k == 0 else -step)) % n * cores + k)
            for y in range(n)
            for k in range(cores)
        ]

    def swap(a):
        pairs = [(y * cores + k, y * cores + 1 - k) for y in range(n) for k in range(cores)]
        return lax.ppermute(a, GROUP, pairs)

    up, down = [own], [own]
    for _ in range(n // 2 - 1):
        up.append(lax.ppermute(up[-1], GROUP, turned(1)))
        down.append(lax.ppermute(down[-1], GROUP, turned(-1)))
    opposite = [lax.ppermute(up[3][:1], GROUP, turned(1)), lax.ppermute(down[3][1:], GROUP, turned(-1))]

    early = jnp.concatenate([up[1], down[1], up[2], down[2], own])
    *opposite, turned_weights = lax.optimization_barrier((*opposite, turned_weights))
    late = jnp.concatenate([up[3], down[3], *opposite])
    return (early, swap(early)), (late, swap(late)), turned_weights


def update_kernel(pieces_ref, w_in_ref, w_out_ref, prec_in_ref, prec_out_ref, *outs, scale):
    total = pieces_ref[0].astype(F32)
    for k in range(1, pieces_ref.shape[0]):
        total += pieces_ref[k].astype(F32)
    width = w_in_ref.shape[1]
    for n, (w_ref, prec_ref) in enumerate(((w_in_ref, prec_in_ref), (w_out_ref, prec_out_ref))):
        grad = total[:, 2 * n * width : (2 * n + 1) * width]
        square = total[:, (2 * n + 1) * width : (2 * n + 2) * width]
        prec = 0.6 * prec_ref[...] + 0.4 * square * scale
        w = w_ref[...].astype(F32)
        outs[n][...] = prec
        outs[2 + n][...] = w - 1.0 * (grad * scale + 0.1 * w) / (prec + 0.1)


def per_device(inputs, cotangent, w_in, w_out, prec_in, prec_out):
    d_own, h_own = w_in.shape
    cols, pairs, deep = (lax.axis_size(a) for a in ("xhi", "xlo", "z"))
    dp = deep * pairs
    hid = cols * h_own
    both = jnp.concatenate([w_in, w_out.T], axis=0)
    both = jnp.broadcast_to(both[None], (cols * dp, *both.shape))
    arrived = lax.all_to_all(both, OWNERS, 0, 0, tiled=True)
    early, late, arrived = round_the_ring(jnp.stack([inputs, cotangent]), arrived)
    core = lax.axis_index("core").reshape(1).astype(jnp.int32)
    partial = [jax.ShapeDtypeStruct((hid, dp * d_own), F32)] * 4
    packed = jax.ShapeDtypeStruct((pairs, cols, deep, d_own, 4 * h_own), BF16)
    turned = jax.ShapeDtypeStruct((2 * hid, dp * d_own), BF16)
    first = functools.partial(first_kernel, pairs=pairs, cols=cols, deep=deep)
    turned, *partial = run_images(first, core, *early, arrived, (), [turned, *partial])
    (pieces,) = run_images(last_kernel, core, *late, turned, tuple(partial), [packed])
    pieces = pieces.reshape(pairs * cols, deep, d_own, 4 * h_own)
    pieces = lax.all_to_all(pieces, ROW, 0, 0, tiled=True)
    pieces = sum(pieces[k].astype(F32) for k in range(cols * pairs)).astype(BF16)
    pieces = lax.all_to_all(pieces, "z", 0, 0, tiled=True)
    images = lax.axis_size("y") * cols * dp
    new_prec_in, new_prec_out, new_w_in, new_w_out = pl.pallas_call(
        functools.partial(update_kernel, scale=1.0 / images),
        out_shape=[jax.ShapeDtypeStruct((d_own, h_own), F32)] * 4,
        compiler_params=pltpu.CompilerParams(vmem_limit_bytes=4 << 20),
    )(pieces, w_in, w_out.T, prec_in, prec_out.T)
    return (new_prec_in, new_prec_out.T, new_w_in, new_w_out.T)


def solution(mesh):
    torus = Mesh(mesh.devices.reshape(8, 2, 2, 8, 2), AXES)
    dp_mp = DP + MP
    in_specs = (P(None, dp_mp), P(None, dp_mp), P(DP, MP), P(MP, DP), P(DP, MP), P(MP, DP))
    out_specs = (P(DP, MP), P(MP, DP), P(DP, MP), P(MP, DP))
    return jax.shard_map(
        per_device, mesh=torus, in_specs=in_specs, out_specs=out_specs, check_vma=False
    )
```

```python
import functools
import math
import jax
import jax.numpy as jnp
from jax import lax
from jax.experimental import pallas as pl
from jax.experimental.pallas import tpu as pltpu
from jax.sharding import Mesh
from jax.sharding import PartitionSpec as P

AXES = ("z", "xlo", "xhi", "y", "core")
DP = ("z", "xlo")
MP = ("xhi", "y", "core")
GROUP = ("y", "core")
OWNERS = ("xlo", "xhi", "z")
ROW = ("xlo", "xhi")
BF16 = jnp.bfloat16
F32 = jnp.float32
ROOT = math.sqrt(2.0 / math.pi)
CUBE = 0.044715
TURN_FLOPS = 1 << 34


def gelu_parts(v):
    v2 = v * v
    t = jnp.tanh(ROOT * v * (1.0 + CUBE * v2))
    half = 0.5 * (1.0 + t)
    slope = half + 0.5 * v * (1.0 - t * t) * (ROOT * (1.0 + 3.0 * CUBE * v2))
    return v * half, slope


def summed(core_ref, own_ref, far_ref, turned_ref):
    first = core_ref[0] == 0
    hid = turned_ref.shape[0] // 2
    last = own_ref.shape[0] // 2 - 1

    def dot(a, b, dims):
        return lax.dot_general(a, b, (dims, ((), ())), preferred_element_type=F32)

    def whole(n, k):
        own = own_ref[2 * n + k]
        far = far_ref[2 * (n ^ 1 if n < last else n) + k]
        return jnp.concatenate(
            [jnp.where(first, own, far), jnp.where(first, far, own)], axis=1
        )

    sums = None
    for n in range(last + 1):
        x, c = whole(n, 0), whole(n, 1)
        pre = dot(turned_ref[:hid], x, ((1,), (1,)))
        back = dot(turned_ref[hid:], c, ((1,), (1,)))
        act, slope = gelu_parts(pre)
        act = act.astype(BF16)
        delta = (back * slope).astype(BF16)
        g_in, g_out = dot(delta, x, ((1,), (0,))), dot(act, c, ((1,), (0,)))
        terms = (g_in, g_in * g_in, g_out, g_out * g_out)
        sums = terms if sums is None else tuple(s + t for s, t in zip(sums, terms))
    return sums


def turn_kernel(arrived_ref, turned_ref, *, pairs, cols, deep):
    own, width = arrived_ref.shape[1] // 2, arrived_ref.shape[2]
    for n in range(2):
        for h in range(cols):
            blocks = [
                arrived_ref[(k % pairs * cols + h) * deep + k // pairs, n * own : (n + 1) * own, :]
                for k in range(deep * pairs)
            ]
            rows = slice((n * cols + h) * width, (n * cols + h + 1) * width)
            turned_ref[rows, :] = jnp.concatenate(blocks, axis=0).T


def first_kernel(core_ref, own_ref, far_ref, arrived_ref, turned_ref, *sums, pairs, cols, deep):
    turn_kernel(arrived_ref, turned_ref, pairs=pairs, cols=cols, deep=deep)
    for ref, term in zip(sums, summed(core_ref, own_ref, far_ref, turned_ref)):
        ref[...] = term


def last_kernel(core_ref, own_ref, far_ref, turned_ref, s0, s1, s2, s3, out_ref):
    sums = summed(core_ref, own_ref, far_ref, turned_ref)
    sums = [ref[...] + term for ref, term in zip((s0, s1, s2, s3), sums)]
    pairs, cols, deep, rows, packed = out_ref.shape
    width = packed // 4
    for h in range(cols):
        part = slice(h * width, (h + 1) * width)
        turned = jnp.concatenate([s[part, :] for s in sums], axis=0).T.astype(BF16)
        for k in range(deep * pairs):
            out_ref[k % pairs, h, k // pairs] = turned[k * rows : (k + 1) * rows]


def run_images(kernel, core, own, far, turned, sums, outs):
    pieces, seq, part = own.shape
    rows, d = (outs[0] if sums == () else turned).shape
    vmem = pl.BlockSpec(memory_space=pltpu.VMEM)
    return pl.pallas_call(
        kernel,
        in_specs=[pl.BlockSpec(memory_space=pltpu.SMEM)] + [vmem] * (3 + len(sums)),
        out_specs=[vmem] * len(outs),
        out_shape=outs,
        compiler_params=pltpu.CompilerParams(vmem_limit_bytes=24 << 20),
        cost_estimate=pl.CostEstimate(
            flops=pieces * 2 * seq * rows * d,
            bytes_accessed=pieces * 4 * seq * part,
            transcendentals=pieces * seq * rows // 4,
        ),
    )(core, own, far, turned, *sums)


def round_the_ring(own, turned_weights):
    n, cores = lax.axis_size("y"), lax.axis_size("core")

    def turned(step):
        return [
            (y * cores + k, (y + (step if k == 0 else -step)) % n * cores + k)
            for y in range(n)
            for k in range(cores)
        ]

    def swap(a):
        pairs = [(y * cores + k, y * cores + 1 - k) for y in range(n) for k in range(cores)]
        return lax.ppermute(a, GROUP, pairs)

    up, down = [own], [own]
    for _ in range(n // 2 - 1):
        up.append(lax.ppermute(up[-1], GROUP, turned(1)))
        down.append(lax.ppermute(down[-1], GROUP, turned(-1)))
    opposite = [lax.ppermute(up[3][:1], GROUP, turned(1)), lax.ppermute(down[3][1:], GROUP, turned(-1))]

    early = jnp.concatenate([up[1], down[1], up[2], down[2], own])
    *opposite, turned_weights = lax.optimization_barrier((*opposite, turned_weights))
    late = jnp.concatenate([up[3], down[3], *opposite])
    return (early, swap(early)), (late, swap(late)), turned_weights


def update_kernel(pieces_ref, w_in_ref, w_out_ref, prec_in_ref, prec_out_ref, *outs, scale):
    total = pieces_ref[0].astype(F32)
    for k in range(1, pieces_ref.shape[0]):
        total += pieces_ref[k].astype(F32)
    width = w_in_ref.shape[1]
    for n, (w_ref, prec_ref) in enumerate(((w_in_ref, prec_in_ref), (w_out_ref, prec_out_ref))):
        grad = total[:, 2 * n * width : (2 * n + 1) * width]
        square = total[:, (2 * n + 1) * width : (2 * n + 2) * width]
        prec = 0.6 * prec_ref[...] + 0.4 * square * scale
        w = w_ref[...].astype(F32)
        outs[n][...] = prec
        outs[2 + n][...] = w - 1.0 * (grad * scale + 0.1 * w) / (prec + 0.1)


def per_device(inputs, cotangent, w_in, w_out, prec_in, prec_out):
    d_own, h_own = w_in.shape
    cols, pairs, deep = (lax.axis_size(a) for a in ("xhi", "xlo", "z"))
    dp = deep * pairs
    hid = cols * h_own
    both = jnp.concatenate([w_in, w_out.T], axis=0)
    both = jnp.broadcast_to(both[None], (cols * dp, *both.shape))
    arrived = lax.all_to_all(both, OWNERS, 0, 0, tiled=True)
    early, late, arrived = round_the_ring(lax.optimization_barrier(jnp.stack([inputs, cotangent])), arrived)
    core = lax.axis_index("core").reshape(1).astype(jnp.int32)
    partial = [jax.ShapeDtypeStruct((hid, dp * d_own), F32)] * 4
    packed = jax.ShapeDtypeStruct((pairs, cols, deep, d_own, 4 * h_own), BF16)
    turned = jax.ShapeDtypeStruct((2 * hid, dp * d_own), BF16)
    first = functools.partial(first_kernel, pairs=pairs, cols=cols, deep=deep)
    turned, *partial = run_images(first, core, *early, arrived, (), [turned, *partial])
    (pieces,) = run_images(last_kernel, core, *late, turned, tuple(partial), [packed])
    pieces = pieces.reshape(pairs * cols, deep, d_own, 4 * h_own)
    pieces = lax.all_to_all(pieces, ROW, 0, 0, tiled=True)
    pieces = sum(pieces[k].astype(F32) for k in range(cols * pairs)).astype(BF16)
    pieces = lax.all_to_all(pieces, "z", 0, 0, tiled=True)
    images = lax.axis_size("y") * cols * dp
    new_prec_in, new_prec_out, new_w_in, new_w_out = pl.pallas_call(
        functools.partial(update_kernel, scale=1.0 / images),
        out_shape=[jax.ShapeDtypeStruct((d_own, h_own), F32)] * 4,
        compiler_params=pltpu.CompilerParams(vmem_limit_bytes=4 << 20),
    )(pieces, w_in, w_out.T, prec_in, prec_out.T)
    return (new_prec_in, new_prec_out.T, new_w_in, new_w_out.T)


def solution(mesh):
    torus = Mesh(mesh.devices.reshape(8, 2, 2, 8, 2), AXES)
    dp_mp = DP + MP
    in_specs = (P(None, dp_mp), P(None, dp_mp), P(DP, MP), P(MP, DP), P(DP, MP), P(MP, DP))
    out_specs = (P(DP, MP), P(MP, DP), P(DP, MP), P(MP, DP))
    return jax.shard_map(
        per_device, mesh=torus, in_specs=in_specs, out_specs=out_specs, check_vma=False
    )
```
